256 devices in a mesh: section: 4 (over y), expert: 64 (over z, x, core).
Axes of the slice: x: 4, y: 4, z: 8, core: 2. Of those that a mesh axis runs over, the one named last changes fastest.
Arguments:
- front_input: bfloat16 [4, 8192, 3584], P('section', 'expert'), may hold values from -6 to 6
- queries: bfloat16 [4, 8192, 3584], P('section', 'expert'), may hold values from -400 to 400
- keys_values: bfloat16 [4, 8192, 448], P('section', 'expert'), may hold values from -6 to 6
- selected_blocks: int32 [4, 128, 2, 4], P('section', 'expert'), may hold values from 0 to 127, as said below
- front_route: int32 [4, 8192, 1], P('section', 'expert'), may hold values from 0 to 15; in each aligned block of 128 rows (0 to 127, 128 to 255, ..., all dimensions but the last counted through in order) at most 9 rows name the same one
- front_gate: float32 [4, 8192, 1], P('section', 'expert'), may hold values from 0.3 to 1
- back_middle: bfloat16 [4, 8192, 3584], P('section', 'expert'), may hold values from -6 to 6
- back_grad: bfloat16 [4, 8192, 3584], P('section', 'expert'), may hold values from -6 to 6
- back_route: int32 [4, 8192, 1], P('section', 'expert'), may hold values from 0 to 15; in each aligned block of 128 rows (0 to 127, 128 to 255, ..., all dimensions but the last counted through in order) at most 9 rows name the same one
- back_gate: float32 [4, 8192, 1], P('section', 'expert'), may hold values from 0.3 to 1
- norm_gain: float32 [4, 3584], P('section'), may hold values from 0.1 to 1.9
- gate_slice: bfloat16 [4, 64, 3584, 256], P('section', 'expert'), may hold values from -0.09375 to 0.09375
- up_slice: bfloat16 [4, 64, 3584, 256], P('section', 'expert'), may hold values from -0.09375 to 0.09375
- down_slice: bfloat16 [4, 64, 256, 3584], P('section', 'expert'), may hold values from -0.1875 to 0.1875
Outputs:
- front_output: bfloat16 [4, 8192, 3584], P('section', 'expert')
- back_output: bfloat16 [4, 8192, 3584], P('section', 'expert')
The draws below stay inside these ranges and needn't reach their ends.
Inputs may be any that keep to these rules, and one draw needn't show every extreme that they name: `selected_blocks`: each list holds 4 different block numbers, among them the query block's own; the others are at most the larger of the query block's number and 3. `front_route`: in the tokens of one device at one section, no expert is named more than 9 times. `back_route`: in the tokens of one device at one section, no expert is named more than 9 times.
All inputs are finite; a program needn't handle non-finite values.
Results may differ from the reference program's by a relative error of at most 0.0057.
Values may be sent and summed in bfloat16 or wider, within the bound.
A program may use at most 192 MiB of HBM per device.

```python
import math
import jax
import jax.numpy as jnp
import numpy as np
from jax import lax

D = 3584
FF = 1024
GROUP = 4
HEADS = 32
HEAD_DIM = 112
KV_HEADS = 2
BLK = 64
SEL = 4
TOP = 1
TOK_DEV = 128
SECTIONS = 4
SLICES = 64
FF_DEV = 256
EXPERTS = 16
TOKENS = 8192
QBLOCKS = 128
CAP = 9
N_SECTION = 4
N_EXPERT = 64


def common_attention_draw(key):
    query_key = jax.random.fold_in(key, 101)
    kv_key = jax.random.fold_in(key, 202)
    kv_width = KV_HEADS * HEAD_DIM
    kv_rows = jax.random.truncated_normal(kv_key, -6.0, 6.0, (N_SECTION, TOKENS, 2 * kv_width), jnp.float32)
    query_rows = jax.random.truncated_normal(query_key, -6.0, 6.0, (N_SECTION, TOKENS, HEADS * HEAD_DIM), jnp.float32)
    return (query_rows, kv_rows)


def draw_queries(key, part):
    return common_attention_draw(key)[0].astype(jnp.bfloat16)


def draw_keys_values(key, part):
    return common_attention_draw(key)[1].astype(jnp.bfloat16)


def draw_selected_blocks(key, part):
    block_count = QBLOCKS
    raw_scores = jax.random.randint(key, (N_SECTION, block_count, KV_HEADS, block_count), 0, 2 ** 16)
    block_ids = jnp.arange(block_count, dtype=jnp.int32)[None, None, None, :]
    query_ids = jnp.arange(block_count, dtype=jnp.int32)[None, :, None, None]
    limit = jnp.maximum(query_ids, SEL - 1)
    scores = raw_scores * block_count + block_ids
    scores = jnp.where(block_ids <= limit, scores, -1 - block_ids)
    scores = jnp.where(block_ids == query_ids, 2 ** 30, scores)
    chosen = lax.top_k(scores, SEL)[1]
    return chosen.astype(jnp.int32)


def level_of(own_key, dims, split, low, top_value):
    loudness, own = 1.0, jax.random.fold_in(own_key, 6)
    for dim, shards_of in split:
        heights = jnp.exp(jax.random.uniform(jax.random.fold_in(own, dim), (shards_of,), jnp.float32, low / len(split), top_value / len(split)))
        loudness = loudness * jnp.repeat(heights, dims[dim] // shards_of).reshape([-1 if axis == dim else 1 for axis in range(len(dims))])
    return loudness


def assign_block(own_key, own, number, rows, number_of, top, most, lean):
    ranking = jax.random.permutation(own_key, number_of)
    packed, ordinary = portions_of(number_of, rows * top, most, lean, True), portions_of(number_of, rows * top, most, lean, False)
    places = jnp.arange(number_of)

    def named(sizes, rotation):
        used = int((sizes > 0).sum())
        fixed = max(1, used // 4)
        passed = fixed + (places - fixed + rotation * (used - fixed)) % max(1, number_of - fixed)
        return jnp.zeros((number_of,), jnp.int32).at[ranking[jnp.where(places < fixed, places, passed)]].set(jnp.asarray(sizes, jnp.int32))

    sizes = jnp.where(number % 4 == 0, named(packed, number // 4), named(ordinary, number - number // 4 - 1))
    mixed = jax.random.permutation(jax.random.fold_in(own, 3), number_of)
    giver, receiver = mixed[0:number_of // 2 * 2:2], mixed[1:number_of // 2 * 2:2]
    slack = jnp.minimum(sizes[giver] - 1, most - sizes[receiver]) // 2
    slack = jnp.where((giver == ranking[0]) | (receiver == ranking[0]) | (sizes[receiver] == 0), 0, jnp.maximum(slack, 0))
    passed = jax.random.randint(jax.random.fold_in(own, 4), (number_of // 2,), 0, 1 << 20) % (slack + 1)
    sizes = sizes.at[giver].add(-passed).at[receiver].add(passed)
    labels = jnp.searchsorted(jnp.cumsum(sizes), jnp.arange(rows * top), side="right").astype(jnp.int32)
    grid = labels.reshape(top, rows).T
    grid = grid[jax.random.permutation(jax.random.fold_in(own, 1), rows)]
    rotation = jax.random.randint(jax.random.fold_in(own, 2), (rows, 1), 0, top)
    return jnp.take_along_axis(grid, (jnp.arange(top)[None, :] + rotation) % top, axis=1)


def portions_of(number_of, total, bound, lean, full):
    weights = [(1 << 20) // math.isqrt(grade ** lean) + 1 for grade in range(1, number_of + 1)]
    largest = bound if full else min(bound, max(-(-total // number_of), total * weights[0] // sum(weights)))
    least = 1 if total - largest >= number_of - 1 else 0
    given, surplus = [largest] + [least] * (number_of - 1), total - largest - least * (number_of - 1)
    while surplus > 0:
        candidates = [i for i in range(1, number_of) if given[i] < largest] or [i for i in range(1, number_of) if given[i] < bound]
        mass, budget = sum([weights[i] for i in candidates]), surplus
        for i in candidates:
            addition = min(bound - given[i], max(1, budget * weights[i] // mass), surplus)
            given[i] = given[i] + addition
            surplus = surplus - addition
    return np.array(given)


def noise(stream_key, shape, width, most, split=(), kind=jnp.bfloat16):
    drawn = jax.random.normal(stream_key, shape, jnp.float32) * width
    if len(split) > 0:
        drawn = level_of(stream_key, shape, split, -0.22, 0.18) * drawn
    return jnp.clip(drawn, min=-most, max=most).astype(kind)


def setup_inputs(seed: int = 0) -> dict:
    streams_of = jax.random.split(jax.random.key(seed), 15)
    front_input = noise(streams_of[0], (SECTIONS, TOKENS, D), 1.0, 6.0, ((0, 4), (1, 64)))
    queries = draw_queries(jax.random.fold_in(streams_of[14], 71), 0)
    keys_values = draw_keys_values(jax.random.fold_in(streams_of[14], 71), 0)
    selected_blocks = draw_selected_blocks(jax.random.fold_in(streams_of[14], 71), 0)
    front_route_keys = jax.random.split(jax.random.fold_in(streams_of[4], 1), SECTIONS * TOKENS // TOK_DEV)
    front_route_turns = jax.random.permutation(jax.random.fold_in(streams_of[4], 3), SECTIONS * TOKENS // TOK_DEV)
    front_route = jax.vmap(lambda own, number: assign_block(jax.random.fold_in(streams_of[4], 2), own, number, TOK_DEV, EXPERTS, TOP, CAP, 2))(front_route_keys, front_route_turns).reshape((SECTIONS, TOKENS, TOP))
    front_gate = jnp.clip(0.3 + 0.7 * jax.random.uniform(streams_of[5], (SECTIONS, TOKENS, TOP), jnp.float32) ** level_of(streams_of[5], (SECTIONS, TOKENS, TOP), ((0, 4), (1, 64)), -0.2, 0.2), 0.3, 1.0)
    back_middle = noise(streams_of[6], (SECTIONS, TOKENS, D), 1.0, 6.0, ((0, 4), (1, 64)))
    back_grad = noise(streams_of[7], (SECTIONS, TOKENS, D), 1.0, 6.0, ((0, 4), (1, 64)))
    back_route_keys = jax.random.split(jax.random.fold_in(streams_of[8], 1), SECTIONS * TOKENS // TOK_DEV)
    back_route_turns = jax.random.permutation(jax.random.fold_in(streams_of[8], 3), SECTIONS * TOKENS // TOK_DEV)
    back_route = jax.vmap(lambda own, number: assign_block(jax.random.fold_in(streams_of[8], 2), own, number, TOK_DEV, EXPERTS, TOP, CAP, 2))(back_route_keys, back_route_turns).reshape((SECTIONS, TOKENS, TOP))
    back_gate = jnp.clip(0.3 + 0.7 * jax.random.uniform(streams_of[9], (SECTIONS, TOKENS, TOP), jnp.float32) ** level_of(streams_of[9], (SECTIONS, TOKENS, TOP), ((0, 4), (1, 64)), -0.2, 0.2), 0.3, 1.0)
    norm_gain = jnp.clip(1.0 + 0.18 * jax.random.normal(streams_of[10], (SECTIONS, D), jnp.float32), 0.1, 1.9)
    gate_slice = noise(streams_of[11], (SECTIONS, SLICES, D, FF_DEV), D ** -0.5, 0.09375, ((0, 4), (1, 64)))
    up_slice = noise(streams_of[12], (SECTIONS, SLICES, D, FF_DEV), D ** -0.5, 0.09375, ((0, 4), (1, 64)))
    down_slice = noise(streams_of[13], (SECTIONS, SLICES, FF_DEV, D), FF ** -0.5, 0.1875, ((0, 4), (1, 64)))
    return dict(front_input=front_input, queries=queries, keys_values=keys_values, selected_blocks=selected_blocks, front_route=front_route, front_gate=front_gate, back_middle=back_middle, back_grad=back_grad, back_route=back_route, back_gate=back_gate, norm_gain=norm_gain, gate_slice=gate_slice, up_slice=up_slice, down_slice=down_slice)


epsilon = 1e-06
negative_large = -1e+30

def rms_scale(rows):
    return lax.rsqrt(lax.optimization_barrier(jnp.mean(rows * rows, axis=-1, keepdims=True)) + epsilon)

def attention(query_rows, kv_rows, chosen_blocks):
    kv_width = KV_HEADS * HEAD_DIM
    block_count = query_rows.shape[0] // BLK
    key_heads = kv_rows[:, :kv_width].reshape(block_count, BLK, KV_HEADS, HEAD_DIM).transpose(2, 0, 1, 3)
    value_heads = kv_rows[:, kv_width:].reshape(block_count, BLK, KV_HEADS, HEAD_DIM).transpose(2, 0, 1, 3)
    groups = HEADS // KV_HEADS
    query_blocks = query_rows.reshape(block_count, BLK, KV_HEADS, groups, HEAD_DIM)
    head_index = jnp.arange(KV_HEADS, dtype=jnp.int32)[:, None]
    offsets = jnp.arange(BLK, dtype=jnp.int32)

    def one_block(bundle):
        query_block, chosen, block_index = bundle
        key_sel = key_heads[head_index, chosen].reshape(KV_HEADS, SEL * BLK, HEAD_DIM).astype(jnp.float32)
        value_sel = value_heads[head_index, chosen].reshape(KV_HEADS, SEL * BLK, HEAD_DIM).astype(jnp.float32)
        scores = jnp.einsum('qhgd,hkd->hgqk', query_block.astype(jnp.float32), key_sel) * HEAD_DIM ** (-0.5)
        key_pos = (chosen[:, :, None] * BLK + offsets[None, None, :]).reshape(KV_HEADS, SEL * BLK)
        query_pos = block_index * BLK + offsets
        allowed = key_pos[:, None, None, :] <= query_pos[None, None, :, None]
        scores = jnp.where(allowed, scores, negative_large)
        row_max = lax.optimization_barrier(jnp.max(scores, axis=-1, keepdims=True))
        exp_scores = jnp.exp(scores - row_max)
        row_total = lax.optimization_barrier(jnp.sum(exp_scores, axis=-1, keepdims=True))
        attention_weights = (exp_scores / row_total).astype(jnp.bfloat16)
        mixed_out = jnp.einsum('hgqk,hkd->qhgd', attention_weights.astype(jnp.float32), value_sel)
        return mixed_out.reshape(BLK, HEADS * HEAD_DIM)
    attended = lax.map(one_block, (query_blocks, chosen_blocks, jnp.arange(block_count, dtype=jnp.int32)))
    return attended.reshape(block_count * BLK, HEADS * HEAD_DIM)

def slot_table(route):
    per_device = route.reshape(N_EXPERT, TOK_DEV * TOP)
    onehot = (per_device[:, :, None] == jnp.arange(EXPERTS, dtype=jnp.int32)[None, None, :]).astype(jnp.int32)
    before = jnp.cumsum(onehot, axis=1) - onehot
    slot_of = lax.optimization_barrier(jnp.sum(before * onehot, axis=2)).astype(jnp.int32)
    source_of = jnp.broadcast_to(jnp.arange(N_EXPERT, dtype=jnp.int32)[:, None], per_device.shape)
    return (per_device, source_of, slot_of)

def dispatch(rows, expert_of, source_of, slot_of):
    buffer = jnp.zeros((EXPERTS, N_EXPERT, CAP, D), rows.dtype)
    return buffer.at[expert_of, source_of, slot_of].set(rows)

def expert_forward(bundle):
    rows, w_gate, w_up, w_down = bundle
    rows = rows.reshape(N_EXPERT * CAP, D)
    total_val = jnp.zeros((N_EXPERT * CAP, D), jnp.float32)
    for slice_index in range(GROUP):
        gate_val = jnp.dot(rows, w_gate[slice_index], preferred_element_type=jnp.float32)
        up_val = jnp.dot(rows, w_up[slice_index], preferred_element_type=jnp.float32)
        hidden = (jax.nn.silu(gate_val) * up_val).astype(jnp.bfloat16)
        partial_value = jnp.dot(hidden, w_down[slice_index], preferred_element_type=jnp.float32).astype(jnp.bfloat16)
        total_val = total_val + partial_value.astype(jnp.float32)
    return total_val.reshape(N_EXPERT, CAP, D)

def expert_backward(bundle):
    rows, grads, w_gate, w_up, w_down = bundle
    rows = rows.reshape(N_EXPERT * CAP, D)
    grads = grads.reshape(N_EXPERT * CAP, D)
    total_val = jnp.zeros((N_EXPERT * CAP, D), jnp.float32)
    for slice_index in range(GROUP):
        gate_val = jnp.dot(rows, w_gate[slice_index], preferred_element_type=jnp.float32)
        up_val = jnp.dot(rows, w_up[slice_index], preferred_element_type=jnp.float32)
        sigmoid_val = jax.nn.sigmoid(gate_val)
        act_val = gate_val * sigmoid_val
        slope_val = sigmoid_val * (1.0 + gate_val * (1.0 - sigmoid_val))
        down_back = jnp.dot(grads, w_down[slice_index].T, preferred_element_type=jnp.float32)
        gate_grad = (down_back * up_val * slope_val).astype(jnp.bfloat16)
        up_grad = (down_back * act_val).astype(jnp.bfloat16)
        slice_grad = jnp.dot(gate_grad, w_gate[slice_index].T, preferred_element_type=jnp.float32)
        slice_grad = slice_grad + jnp.dot(up_grad, w_up[slice_index].T, preferred_element_type=jnp.float32)
        total_val = total_val + slice_grad.astype(jnp.bfloat16).astype(jnp.float32)
    return total_val.reshape(N_EXPERT, CAP, D)

def reference(front_input, queries, keys_values, selected_blocks, front_route, front_gate, back_middle, back_grad, back_route, back_gate, norm_gain, gate_slice, up_slice, down_slice):
    front_list = []
    back_list = []
    for section_index in range(N_SECTION):
        gain_row = norm_gain[section_index]
        w_gate = gate_slice[section_index].reshape(EXPERTS, GROUP, D, FF_DEV)
        w_up = up_slice[section_index].reshape(EXPERTS, GROUP, D, FF_DEV)
        w_down = down_slice[section_index].reshape(EXPERTS, GROUP, FF_DEV, D)
        attention_out = attention(queries[section_index], keys_values[section_index], selected_blocks[section_index])
        middle = (front_input[section_index].astype(jnp.float32) + attention_out).astype(jnp.bfloat16)
        middle = lax.optimization_barrier(middle).astype(jnp.float32)
        normed = (middle * rms_scale(middle) * gain_row).astype(jnp.bfloat16)
        expert_of, source_of, slot_of = slot_table(front_route[section_index])
        rows = jnp.repeat(normed.reshape(N_EXPERT, TOK_DEV, D), TOP, axis=1)
        buffer = dispatch(rows, expert_of, source_of, slot_of)
        expert_out = lax.map(expert_forward, (buffer, w_gate, w_up, w_down))
        picked = expert_out[expert_of, source_of, slot_of]
        weighted = picked * front_gate[section_index].reshape(N_EXPERT, TOK_DEV * TOP)[:, :, None]
        contrib = lax.optimization_barrier(jnp.sum(weighted.reshape(TOKENS, TOP, D), axis=1))
        front_list.append((middle + contrib).astype(jnp.bfloat16))
        back_mid = back_middle[section_index].astype(jnp.float32)
        back_scale = rms_scale(back_mid)
        back_normed = (back_mid * back_scale * gain_row).astype(jnp.bfloat16)
        expert_of, source_of, slot_of = slot_table(back_route[section_index])
        grad_rows = jnp.repeat(back_grad[section_index].astype(jnp.float32), TOP, axis=0)
        scaled = (back_gate[section_index].reshape(TOKENS * TOP, 1) * grad_rows).astype(jnp.bfloat16)
        rows = jnp.repeat(back_normed.reshape(N_EXPERT, TOK_DEV, D), TOP, axis=1)
        buffer_rows = dispatch(rows, expert_of, source_of, slot_of)
        buffer_grads = dispatch(scaled.reshape(N_EXPERT, TOK_DEV * TOP, D), expert_of, source_of, slot_of)
        expert_grad = lax.map(expert_backward, (buffer_rows, buffer_grads, w_gate, w_up, w_down))
        picked = expert_grad[expert_of, source_of, slot_of]
        normed_grad = lax.optimization_barrier(jnp.sum(picked.reshape(TOKENS, TOP, D), axis=1))
        amount = gain_row * normed_grad
        cube = back_scale * back_scale * back_scale
        back_result = back_grad[section_index].astype(jnp.float32) + back_scale * amount - back_mid * cube * lax.optimization_barrier(jnp.mean(back_mid * amount, axis=-1, keepdims=True))
        back_list.append(back_result.astype(jnp.bfloat16))
    front_output = jnp.roll(jnp.stack(front_list), 1, axis=0)
    back_output = jnp.roll(jnp.stack(back_list), -1, axis=0)
    return (front_output, back_output)
```

```python
import functools

import jax
import jax.numpy as jnp
from jax import lax
from jax.experimental import pallas as pl
from jax.experimental.pallas import tpu as pltpu
from jax.sharding import PartitionSpec as P

HEADS = 32
HEAD_DIM = 112
KV_HEADS = 2
GROUPS = HEADS // KV_HEADS
BLK = 64
SEL = 4
QUARTERS = 4
NX = 4
EPS = 1e-06
NEG = -1e30
MESH = pl.DeviceIdType.MESH
BF = jnp.bfloat16
F32 = jnp.float32


def iota(shape, dim):
    return lax.broadcasted_iota(jnp.int32, shape, dim)


def slot_row(route, experts):
    tokens = route.shape[1]
    onehot = jnp.where(iota((experts, tokens), 0) == route, 1.0, 0.0)
    earlier = jnp.where(iota((tokens, tokens), 0) < iota((tokens, tokens), 1), 1.0, 0.0)
    before = jnp.dot(onehot.astype(BF), earlier.astype(BF), preferred_element_type=F32)
    return jnp.sum(before * onehot, axis=0, keepdims=True).astype(jnp.int32)


def main_onehot(route, slot, experts):
    place = jnp.where(slot < 8, route * 8 + slot, -1)
    return jnp.where(iota((experts * 8, route.shape[1]), 0) == place, 1.0, 0.0)


def tail_onehot(route, slot, experts, quarter):
    place = jnp.where(slot >= 8, route * 4 + quarter, -1)
    return jnp.where(iota((experts * 4, route.shape[1]), 0) == place, 1.0, 0.0)


def pack(route, experts, rows_of, send_ref):
    slot = slot_row(route, experts)
    main = main_onehot(route, slot, experts).astype(BF)
    planes = experts // 2
    tail = None
    for q in range(QUARTERS):
        rows = rows_of(q)
        width = rows.shape[1]
        sorted_rows = jnp.dot(main, rows, preferred_element_type=F32).reshape(planes, 2, 8, width)
        send_ref[:, q] = sorted_rows[:, 0].astype(BF)
        send_ref[:, 5 + q] = sorted_rows[:, 1].astype(BF)
        last = jnp.dot(
            tail_onehot(route, slot, experts, q).astype(BF), rows, preferred_element_type=F32
        )
        tail = last if tail is None else tail + last
    send_ref[:, 4] = tail.reshape(planes, 8, width).astype(BF)


def unpack(route, experts, back_ref):
    slot = slot_row(route, experts)
    main = main_onehot(route, slot, experts).T.astype(BF)
    planes = experts // 2
    width = back_ref.shape[3]

    def rows_of(q):
        first = back_ref[:, q].astype(F32)
        second = back_ref[:, 5 + q].astype(F32)
        both = jnp.stack([first, second], axis=1).reshape(experts * 8, width).astype(BF)
        last = back_ref[:, 4].astype(F32).reshape(planes * 8, width).astype(BF)
        tail = tail_onehot(route, slot, experts, q).T.astype(BF)
        return jnp.dot(main, both, preferred_element_type=F32) + jnp.dot(
            tail, last, preferred_element_type=F32
        )

    return rows_of


def quarter(q, width):
    return slice(q * width, (q + 1) * width)


def back_pack_kernel(mid_ref, grad_ref, gain_ref, gate_ref, route_ref, rows_ref, grads_ref):
    experts = rows_ref.shape[0] * 2
    width = rows_ref.shape[3]
    mid = mid_ref[...].astype(F32)
    scale = lax.rsqrt(jnp.mean(mid * mid, axis=-1, keepdims=True) + EPS)
    tokens = mid.shape[0]
    gate = jnp.broadcast_to(gate_ref[...], (tokens, tokens)).T[:, 0:1]
    route = route_ref[...]

    def normed(q):
        part = mid_ref[:, quarter(q, width)].astype(F32)
        return (part * scale * gain_ref[:, quarter(q, width)]).astype(BF)

    def scaled(q):
        return (gate * grad_ref[:, quarter(q, width)].astype(F32)).astype(BF)

    pack(route, experts, normed, rows_ref)
    pack(route, experts, scaled, grads_ref)


def attention_kernel(
    sel_ref, query_ref, kv_ref, input_ref, gain_ref, route_ref,
    middle_ref, send_ref, kbuf, vbuf, total, sem,
):
    experts = send_ref.shape[0] * 2
    width = send_ref.shape[3]
    tokens = query_ref.shape[0]
    blocks = tokens // BLK
    first = sel_ref[blocks * KV_HEADS * SEL]
    copies = []
    for b in range(blocks):
        for h in range(KV_HEADS):
            for k in range(SEL):
                index = (b * KV_HEADS + h) * SEL + k
                chosen = sel_ref[index]
                owner = chosen // blocks
                rows = pl.ds(pl.multiple_of((chosen % blocks) * BLK, BLK), BLK)
                for w, buf in enumerate((kbuf, vbuf)):
                    copy = pltpu.make_async_copy(
                        kv_ref.at[owner, 2 * w + h, rows],
                        buf.at[b * KV_HEADS + h, pl.ds(k * BLK, BLK)],
                        sem.at[w, index],
                    )
                    copy.start()
                    copies.append(copy)
    total[...] = jnp.zeros_like(total)
    for copy in copies:
        copy.wait()
    keys = SEL * BLK
    for b in range(blocks):
        token_rows = slice(b * BLK, (b + 1) * BLK)
        query_pos = (first + b) * BLK + iota((2 * BLK, keys), 0) % BLK
        for h in range(KV_HEADS):
            pair = b * KV_HEADS + h
            lane = iota((2 * BLK, keys), 1)
            key_pos = lane % BLK
            for k in range(SEL):
                key_pos = key_pos + jnp.where(
                    lane // BLK == k, sel_ref[pair * SEL + k] * BLK, 0
                )
            allowed = key_pos <= query_pos
            key_rows = kbuf[pair]
            value_rows = vbuf[pair]
            for g in range(GROUPS // 2):
                offset = (HEAD_DIM * g) % 128
                window = 128 if offset + HEAD_DIM <= 128 else 256
                at = iota((128, window), 0)
                shift = jnp.where(
                    (iota((128, window), 1) == at + offset) & (at < HEAD_DIM), 1.0, 0.0
                ).astype(BF)
                key_moved = jnp.dot(key_rows, shift, preferred_element_type=F32).astype(BF)
                value_moved = jnp.dot(value_rows, shift, preferred_element_type=F32).astype(BF)
                starts = []
                for half in range(2):
                    head = h * GROUPS + g + half * (GROUPS // 2)
                    starts.append(HEAD_DIM * head // 128 * 128)
                query = jnp.concatenate(
                    [query_ref[token_rows, s : s + window] for s in starts], axis=0
                )
                scores = lax.dot_general(
                    query, key_moved, (((1,), (1,)), ((), ())), preferred_element_type=F32
                ) * HEAD_DIM ** (-0.5)
                scores = jnp.where(allowed, scores, NEG)
                exp_scores = jnp.exp(scores - jnp.max(scores, axis=-1, keepdims=True))
                weights = exp_scores / jnp.sum(exp_scores, axis=-1, keepdims=True)
                mixed = jnp.dot(weights.astype(BF), value_moved, preferred_element_type=F32)
                for half, s in enumerate(starts):
                    total[token_rows, s : s + window] += mixed[half * BLK : (half + 1) * BLK]
    squares = jnp.zeros((tokens, 1), F32)
    for q in range(QUARTERS):
        cols = quarter(q, width)
        middle = (input_ref[:, cols].astype(F32) + total[:, cols]).astype(BF)
        middle_ref[:, cols] = middle
        middle = middle.astype(F32)
        squares += jnp.sum(middle * middle, axis=-1, keepdims=True)
    scale = lax.rsqrt(squares / query_ref.shape[1] + EPS)

    def normed(q):
        cols = quarter(q, width)
        return (middle_ref[:, cols].astype(F32) * scale * gain_ref[:, cols]).astype(BF)

    pack(route_ref[...], experts, normed, send_ref)


def tail_select(count, h, q):
    row, col = iota((count, count * 8), 0), iota((count, count * 8), 1)
    return jnp.where(col == row * 8 + h * 4 + q, 1.0, 0.0).astype(BF)


def rows_for_expert(recv_ref, h, q):
    count, width = recv_ref.shape[0], recv_ref.shape[3]
    main = recv_ref[:, q + h].astype(F32).reshape(count * 8, width).astype(BF)
    last = recv_ref[:, 4 - 4 * h].astype(F32).reshape(count * 8, width).astype(BF)
    tail = jnp.dot(tail_select(count, h, q), last, preferred_element_type=F32).astype(BF)
    return jnp.concatenate([main, tail], axis=0)


def store_for_source(out_ref, h, q, value, tail_total):
    count, width = out_ref.shape[0], out_ref.shape[3]
    out_ref[:, q + h] = value[: count * 8].reshape(count, 8, width).astype(BF)
    spread = lax.dot_general(
        tail_select(count, h, q), value[count * 8 :].astype(BF),
        (((0,), (0,)), ((), ())), preferred_element_type=F32,
    )
    return spread if tail_total is None else tail_total + spread


def forward_kernel(h_ref, recv_ref, g0, u0, d0, g1, u1, d1, out_ref):
    h = h_ref[0]
    width = recv_ref.shape[3]
    sides = ((g0, u0, d0), (g1, u1, d1))
    gates, ups = [None, None], [None, None]
    for q in range(QUARTERS):
        rows = rows_for_expert(recv_ref, h, q)
        part = quarter(q, width)
        for i, (g, u, _) in enumerate(sides):
            gate = jnp.dot(rows, g[part], preferred_element_type=F32)
            up = jnp.dot(rows, u[part], preferred_element_type=F32)
            gates[i] = gate if gates[i] is None else gates[i] + gate
            ups[i] = up if ups[i] is None else ups[i] + up
    hidden = [(v / (1.0 + jnp.exp(-v)) * u).astype(BF) for v, u in zip(gates, ups)]
    tail = None
    for q in range(QUARTERS):
        part = quarter(q, width)
        value = jnp.dot(hidden[0], d0[:, part], preferred_element_type=F32) + jnp.dot(
            hidden[1], d1[:, part], preferred_element_type=F32
        )
        tail = store_for_source(out_ref, h, q, value, tail)
    out_ref[:, 4 - 4 * h] = tail.reshape(out_ref.shape[0], 8, width).astype(BF)


def backward_kernel(h_ref, recv_ref, recv_grad_ref, g0, u0, d0, g1, u1, d1, out_ref):
    h = h_ref[0]
    width = recv_ref.shape[3]
    last = (((1,), (1,)), ((), ()))
    sides = ((g0, u0, d0), (g1, u1, d1))
    gates, ups, downs = [None, None], [None, None], [None, None]
    for q in range(QUARTERS):
        rows = rows_for_expert(recv_ref, h, q)
        grads = rows_for_expert(recv_grad_ref, h, q)
        part = quarter(q, width)
        for i, (g, u, d) in enumerate(sides):
            gate = jnp.dot(rows, g[part], preferred_element_type=F32)
            up = jnp.dot(rows, u[part], preferred_element_type=F32)
            down = lax.dot_general(grads, d[:, part], last, preferred_element_type=F32)
            gates[i] = gate if gates[i] is None else gates[i] + gate
            ups[i] = up if ups[i] is None else ups[i] + up
            downs[i] = down if downs[i] is None else downs[i] + down
    gate_grads, up_grads = [], []
    for gate, up, down in zip(gates, ups, downs):
        sigmoid = 1.0 / (1.0 + jnp.exp(-gate))
        gate_grads.append((down * up * (sigmoid * (1.0 + gate * (1.0 - sigmoid)))).astype(BF))
        up_grads.append((down * (gate * sigmoid)).astype(BF))
    tail = None
    for q in range(QUARTERS):
        part = quarter(q, width)
        value = None
        for i, (g, u, _) in enumerate(sides):
            more = lax.dot_general(
                gate_grads[i], g[part], last, preferred_element_type=F32
            ) + lax.dot_general(up_grads[i], u[part], last, preferred_element_type=F32)
            value = more if value is None else value + more
        tail = store_for_source(out_ref, h, q, value, tail)
    out_ref[:, 4 - 4 * h] = tail.reshape(out_ref.shape[0], 8, width).astype(BF)


def front_last_kernel(middle_ref, back_ref, meta_ref, out_ref):
    experts = back_ref.shape[0] * 2
    width = back_ref.shape[3]
    tokens = middle_ref.shape[0]
    gate = jnp.broadcast_to(meta_ref[0:1], (tokens, tokens)).T[:, 0:1]
    rows_of = unpack(meta_ref[1:2].astype(jnp.int32), experts, back_ref)
    for q in range(QUARTERS):
        cols = quarter(q, width)
        out_ref[:, cols] = (middle_ref[:, cols].astype(F32) + gate * rows_of(q)).astype(BF)


def back_last_kernel(mid_ref, grad_ref, gain_ref, back_ref, meta_ref, out_ref, amount):
    experts = back_ref.shape[0] * 2
    width = back_ref.shape[3]
    features = mid_ref.shape[1]
    rows_of = unpack(meta_ref[1:2].astype(jnp.int32), experts, back_ref)
    tokens = mid_ref.shape[0]
    squares = jnp.zeros((tokens, 1), F32)
    products = jnp.zeros((tokens, 1), F32)
    for q in range(QUARTERS):
        cols = quarter(q, width)
        mid = mid_ref[:, cols].astype(F32)
        value = gain_ref[:, cols] * rows_of(q)
        amount[:, cols] = value
        squares += jnp.sum(mid * mid, axis=-1, keepdims=True)
        products += jnp.sum(mid * value, axis=-1, keepdims=True)
    scale = lax.rsqrt(squares / features + EPS)
    factor = scale * scale * scale * (products / features)
    for q in range(QUARTERS):
        cols = quarter(q, width)
        out_ref[:, cols] = (
            grad_ref[:, cols].astype(F32)
            + scale * amount[:, cols]
            - mid_ref[:, cols].astype(F32) * factor
        ).astype(BF)


def place():
    section, index = lax.axis_index("section"), lax.axis_index("expert")
    return section, index // (2 * NX), (index // 2) % NX, index % 2


def device(section, z, x, core):
    return (section, (z * NX + x) * 2 + core)


def far_first(planes):
    near = sorted(range(1, planes), key=lambda d: -min(d, planes - d))
    return near


def near_first(planes):
    return sorted(range(1, planes), key=lambda d: min(d, planes - d))


def greet(targets):
    barrier = pltpu.get_barrier_semaphore()
    for target in targets:
        pl.semaphore_signal(barrier, inc=1, device_id=target, device_id_type=MESH)
    pl.semaphore_wait(barrier, len(targets))


def remote(src, dst, send, recv, target):
    return pltpu.make_async_remote_copy(
        src_ref=src, dst_ref=dst, send_sem=send, recv_sem=recv,
        device_id=target, device_id_type=MESH,
    )


class Dispatch:
    def __init__(self, send_ref, zbuf, out_ref, zsend, zrecv, xsend, xrecv, local):
        self.refs = (send_ref, zbuf, out_ref)
        self.sems = (zsend, zrecv, xsend, xrecv, local)
        self.planes = send_ref.shape[0]
        self.started = []

    def start(self):
        send_ref, zbuf, _ = self.refs
        zsend, zrecv, _, _, local = self.sems
        s, z, x, c = place()
        for d in far_first(self.planes):
            to = (z + d) % self.planes
            copy = remote(
                send_ref.at[to], zbuf.at[z], zsend.at[d], zrecv.at[z], device(s, to, x, c)
            )
            copy.start()
            self.started.append(copy)
        self.own = pltpu.make_async_copy(send_ref.at[z], zbuf.at[z], local.at[self.planes])
        self.own.start()

    def forward(self, d):
        send_ref, zbuf, out_ref = self.refs
        zsend, zrecv, xsend, xrecv, local = self.sems
        s, z, x, c = place()
        origin = (z + d) % self.planes
        if d == 0:
            self.own.wait()
        else:
            remote(
                send_ref.at[origin], zbuf.at[origin], zsend.at[d], zrecv.at[origin],
                device(s, origin, x, c),
            ).wait_recv()
        for dx in (2, 1, 3):
            to = (x + dx) % NX
            copy = remote(
                zbuf.at[origin, pl.ds(4 * (to // 2), 5)], out_ref.at[x, origin],
                xsend.at[dx - 1, d], xrecv.at[x, origin], device(s, z, to, c),
            )
            copy.start()
            self.started.append(copy)
        mine = pltpu.make_async_copy(
            zbuf.at[origin, pl.ds(4 * (x // 2), 5)], out_ref.at[x, origin], local.at[d]
        )
        mine.start()
        self.started.append(mine)

    def finish(self):
        send_ref, zbuf, out_ref = self.refs
        zsend, zrecv, xsend, xrecv, local = self.sems
        s, z, x, c = place()
        for d in range(self.planes):
            origin = (z + d) % self.planes
            for dx in range(1, NX):
                source = (x + dx) % NX
                remote(
                    zbuf.at[origin, pl.ds(0, 5)], out_ref.at[source, origin],
                    xsend.at[dx - 1, d], xrecv.at[source, origin], device(s, z, source, c),
                ).wait_recv()
        for copy in self.started:
            if hasattr(copy, "wait_send") and copy.is_remote:
                copy.wait_send()
            else:
                copy.wait()

    @staticmethod
    def scratch(planes, width):
        dma = pltpu.SemaphoreType.DMA
        return [
            pltpu.VMEM((planes, 9, 8, width), BF),
            dma((planes,)), dma((planes,)), dma((NX - 1, planes)), dma((NX, planes)),
            dma((planes + 1,)),
        ]


class Return:
    def __init__(self, part_ref, pbuf, stage, out_ref, xsend, xrecv, zsend, zrecv, local, by):
        self.refs = (part_ref, pbuf, stage, out_ref)
        self.sems = (xsend, xrecv, zsend, zrecv, local)
        self.planes = part_ref.shape[1]
        self.by = by
        self.started = []

    def order(self):
        return far_first(self.planes) + [0]

    def start(self):
        part_ref, pbuf, _, _ = self.refs
        xsend, xrecv, _, _, local = self.sems
        s, z, x, c = place()
        self.own = {}
        for d in self.order():
            origin = (z + d) % self.planes
            for dx in (2, 1, 3):
                to = (x + dx) % NX
                copy = remote(
                    part_ref.at[to, origin], pbuf.at[x, origin],
                    xsend.at[dx - 1, d], xrecv.at[x, origin], device(s, z, to, c),
                )
                copy.start()
                self.started.append(copy)
            self.own[d] = pltpu.make_async_copy(
                part_ref.at[x, origin], pbuf.at[x, origin], local.at[d]
            )
            self.own[d].start()

    def forward(self, d):
        part_ref, pbuf, stage, out_ref = self.refs
        xsend, xrecv, zsend, zrecv, local = self.sems
        s, z, x, c = place()
        origin = (z + d) % self.planes
        self.own[d].wait()
        for dx in range(1, NX):
            source = (x + dx) % NX
            remote(
                part_ref.at[source, origin], pbuf.at[source, origin],
                xsend.at[dx - 1, d], xrecv.at[source, origin], device(s, z, source, c),
            ).wait_recv()
        for k in range(4):
            stage[origin, k] = (
                pbuf[0, origin, k].astype(F32) + pbuf[1, origin, k].astype(F32)
            ).astype(BF)
            stage[origin, 5 + k] = (
                pbuf[2, origin, 1 + k].astype(F32) + pbuf[3, origin, 1 + k].astype(F32)
            ).astype(BF)
        stage[origin, 4] = (
            (pbuf[0, origin, 4].astype(F32) + pbuf[1, origin, 4].astype(F32))
            + (pbuf[2, origin, 0].astype(F32) + pbuf[3, origin, 0].astype(F32))
        ).astype(BF)
        sections = lax.axis_size("section")
        copy = remote(
            stage.at[origin], out_ref.at[z], zsend.at[d], zrecv.at[z],
            device((s + self.by + sections) % sections, origin, x, c),
        )
        copy.start()
        self.started.append(copy)

    def finish(self):
        part_ref, pbuf, stage, out_ref = self.refs
        xsend, xrecv, zsend, zrecv, local = self.sems
        s, z, x, c = place()
        sections = lax.axis_size("section")
        for d in range(self.planes):
            origin = (z + d) % self.planes
            remote(
                stage.at[origin], out_ref.at[origin], zsend.at[d], zrecv.at[origin],
                device((s - self.by + sections) % sections, origin, x, c),
            ).wait_recv()
        for copy in self.started:
            copy.wait_send()

    @staticmethod
    def scratch(planes, width):
        dma = pltpu.SemaphoreType.DMA
        return [
            pltpu.VMEM((NX, planes, 5, 8, width), BF),
            pltpu.VMEM((planes, 9, 8, width), BF),
            dma((NX - 1, planes)), dma((NX, planes)), dma((planes,)), dma((planes,)),
            dma((planes,)),
        ]


def row_peers(planes):
    s, z, x, c = place()
    peers = [device(s, (z + d) % planes, x, c) for d in range(1, planes)]
    return peers + [device(s, z, (x + d) % NX, c) for d in range(1, NX)]


def section_peers(planes, sections):
    s, z, x, c = place()
    return [
        device((s + by) % sections, (z + d) % planes, x, c)
        for by in (1, sections - 1) for d in range(planes)
    ]


def swap(refs, outs, send, recv, target):
    copies = []
    for i, (ref, out) in enumerate(zip(refs, outs)):
        copy = remote(ref, out, send.at[i], recv.at[i], target)
        copy.start()
        copies.append(copy)
    return copies


def kernel_a(
    rows_ref, grads_ref, wg, wu, wd, mid, grad, gain, meta,
    rows_out, grads_out, pg, pu, pd, mid_out, grad_out, gain_out, meta_out,
    *scratch,
):
    half = (len(scratch) - 2) // 2
    s, z, x, c = place()
    sections = lax.axis_size("section")
    planes = rows_ref.shape[0]
    before = device((s + sections - 1) % sections, z, x, c)
    after = device((s + 1) % sections, z, x, c)
    core = device(s, z, x, 1 - c)
    greet(row_peers(planes) + [before, after, core])
    send, recv = scratch[-2:]
    ones = Dispatch(rows_ref, scratch[0], rows_out, *scratch[1:half])
    twos = Dispatch(grads_ref, scratch[half], grads_out, *scratch[half + 1 : 2 * half])
    ones.start()
    twos.start()
    copies = swap((wg, wu, wd), (pg, pu, pd), send.at[0], recv.at[0], core)
    copies += swap(
        (mid, grad, gain, meta), (mid_out, grad_out, gain_out, meta_out),
        send.at[1], recv.at[1], before,
    )
    for one in (ones, twos):
        for d in [0] + near_first(planes):
            one.forward(d)
    ones.finish()
    twos.finish()
    for copy in copies:
        copy.wait()


def kernel_b(send_ref, part_ref, middle, meta, rows_out, back_out, middle_out, meta_out, *scratch):
    s, z, x, c = place()
    sections = lax.axis_size("section")
    planes = send_ref.shape[0]
    greet(row_peers(planes) + section_peers(planes, sections))
    front = Dispatch(send_ref, scratch[0], rows_out, *scratch[1:6])
    back = Return(part_ref, scratch[6], scratch[7], back_out, *scratch[8:13], -1)
    send, recv = scratch[-2:]
    front.start()
    back.start()
    copies = swap(
        (middle, meta), (middle_out, meta_out), send, recv,
        device((s + 1) % sections, z, x, c),
    )
    for d, b in zip([0] + near_first(planes), back.order()):
        back.forward(b)
        front.forward(d)
    front.finish()
    back.finish()
    for copy in copies:
        copy.wait()


def kernel_c(part_ref, back_out, *scratch):
    planes = part_ref.shape[1]
    s, z, x, c = place()
    sections = lax.axis_size("section")
    greet(row_peers(planes)[planes - 1 :] + section_peers(planes, sections))
    front = Return(part_ref, scratch[0], scratch[1], back_out, *scratch[2:7], 1)
    front.start()
    for d in front.order():
        front.forward(d)
    front.finish()


ANY = pl.BlockSpec(memory_space=pl.ANY)
VMEM = pl.BlockSpec(memory_space=pltpu.VMEM)
SMEM = pl.BlockSpec(memory_space=pltpu.SMEM)


def like(*arrays):
    return [jax.ShapeDtypeStruct(a.shape, a.dtype) for a in arrays]


def speak(kernel, number, out_shape, scratch, *args):
    return pl.pallas_call(
        kernel,
        out_shape=out_shape,
        in_specs=[ANY] * len(args),
        out_specs=[ANY] * len(out_shape),
        scratch_shapes=scratch,
        compiler_params=pltpu.CompilerParams(
            collective_id=number, has_side_effects=True, vmem_limit_bytes=24 << 20
        ),
    )(*args)


def compute(kernel, out_shape, *args, specs=None, scratch=(), mib=48):
    return pl.pallas_call(
        kernel,
        out_shape=out_shape,
        in_specs=specs or [VMEM] * len(args),
        out_specs=jax.tree.map(lambda _: VMEM, out_shape),
        scratch_shapes=list(scratch),
        compiler_params=pltpu.CompilerParams(vmem_limit_bytes=mib << 20),
    )(*args)


def shards(
    front_input, queries, keys_values, selected_blocks, front_route, front_gate,
    back_middle, back_grad, back_route, back_gate, norm_gain, gate_slice, up_slice, down_slice,
):
    tokens, features = front_input.shape[1:]
    planes = lax.axis_size("expert") // (2 * NX)
    width = features // QUARTERS
    wg, wu, wd = gate_slice[0, 0], up_slice[0, 0], down_slice[0, 0]
    mid, grad, entry = back_middle[0], back_grad[0], front_input[0]
    f_route = front_route.reshape(1, tokens)
    b_route = back_route.reshape(1, tokens)
    f_meta = jnp.concatenate(
        [front_gate.reshape(1, tokens), f_route.astype(F32), jnp.zeros((6, tokens), F32)]
    )
    b_meta = jnp.concatenate(
        [back_gate.reshape(1, tokens), b_route.astype(F32), jnp.zeros((6, tokens), F32)]
    )
    kv = keys_values[0].reshape(tokens, 2 * KV_HEADS, HEAD_DIM).transpose(1, 0, 2)
    kv = jnp.pad(kv, ((0, 0), (0, 0), (0, 128 - HEAD_DIM)))
    gathered = lax.all_gather(kv, "expert")
    index = lax.axis_index("expert")
    half = ((index // 4) % 2).astype(jnp.int32).reshape(1)
    message = jax.ShapeDtypeStruct((planes, 9, 8, width), BF)
    arrived = jax.ShapeDtypeStruct((NX, planes, 5, 8, width), BF)
    flat = jax.ShapeDtypeStruct((NX * planes, 5, 8, width), BF)
    dma = pltpu.SemaphoreType.DMA

    with jax.named_scope("back_pack"):
        back_rows, back_grads = compute(
            back_pack_kernel, [message, message], mid, grad, norm_gain,
            back_gate.reshape(1, tokens), b_route,
        )
    with jax.named_scope("exchange_a"):
        (rows_in, grads_in, pg, pu, pd, mid_in, grad_in, gain_in, b_meta_in) = speak(
            kernel_a, 0, [arrived, arrived] + like(wg, wu, wd, mid, grad, norm_gain, b_meta),
            Dispatch.scratch(planes, width) * 2 + [dma((2, 4)), dma((2, 4))],
            back_rows, back_grads, wg, wu, wd, mid, grad, norm_gain, b_meta,
        )
    with jax.named_scope("attention"):
        blocks = tokens // BLK
        picks = jnp.concatenate(
            [selected_blocks.reshape(-1), (index * blocks).astype(jnp.int32).reshape(1)]
        )
        middle, front_rows = compute(
            attention_kernel,
            [jax.ShapeDtypeStruct((tokens, features), BF), message],
            picks, queries[0], gathered, entry, norm_gain, f_route,
            specs=[SMEM, VMEM, ANY, VMEM, VMEM, VMEM],
            scratch=[
                pltpu.VMEM((blocks * KV_HEADS, SEL * BLK, 128), BF),
                pltpu.VMEM((blocks * KV_HEADS, SEL * BLK, 128), BF),
                pltpu.VMEM((tokens, features), F32),
                dma((2, blocks * KV_HEADS * SEL)),
            ],
        )
    weights = (wg, wu, wd, pg, pu, pd)
    with jax.named_scope("backward_experts"):
        back_part = compute(
            backward_kernel, flat, half, rows_in.reshape(flat.shape),
            grads_in.reshape(flat.shape), *weights, specs=[SMEM] + [VMEM] * 8,
        )
    with jax.named_scope("exchange_b"):
        rows_in, back_out, middle_in, f_meta_in = speak(
            kernel_b, 1, [arrived, message] + like(middle, f_meta),
            Dispatch.scratch(planes, width) + Return.scratch(planes, width) + [dma((2,)), dma((2,))],
            front_rows, back_part.reshape(arrived.shape), middle, f_meta,
        )
    with jax.named_scope("forward_experts"):
        front_part = compute(
            forward_kernel, flat, half, rows_in.reshape(flat.shape), *weights,
            specs=[SMEM] + [VMEM] * 7,
        )
    with jax.named_scope("back_last"):
        back_output = compute(
            back_last_kernel, jax.ShapeDtypeStruct((tokens, features), BF),
            mid_in, grad_in, gain_in, back_out, b_meta_in,
            scratch=[pltpu.VMEM((tokens, features), F32)],
        )
    with jax.named_scope("exchange_c"):
        (front_out,) = speak(
            kernel_c, 2, [message], Return.scratch(planes, width),
            front_part.reshape(arrived.shape),
        )
    with jax.named_scope("front_last"):
        front_output = compute(
            front_last_kernel, jax.ShapeDtypeStruct((tokens, features), BF),
            middle_in, front_out, f_meta_in,
        )
    return (front_output[None], back_output[None])


def solution(mesh):
    rows = P("section", "expert", None)
    wide = P("section", "expert", None, None)
    return jax.shard_map(
        shards,
        mesh=mesh,
        in_specs=(rows, rows, rows, wide, rows, rows, rows, rows, rows, rows,
                  P("section", None), wide, wide, wide),
        out_specs=(rows, rows),
        check_vma=False,
    )
```

```python
import jax
import jax.numpy as jnp
from jax import lax
from jax.experimental import pallas as pl
from jax.experimental.pallas import tpu as pltpu
from jax.sharding import PartitionSpec as P

HEADS = 32
HEAD_DIM = 112
KV_HEADS = 2
GROUPS = HEADS // KV_HEADS
BLK = 64
SEL = 4
QUARTERS = 4
NX = 4
EPS = 1e-06
NEG = -1e30
MESH = pl.DeviceIdType.MESH
BF = jnp.bfloat16
F32 = jnp.float32


def iota(shape, dim):
    return lax.broadcasted_iota(jnp.int32, shape, dim)


def slot_row(route, experts):
    tokens = route.shape[1]
    onehot = jnp.where(iota((experts, tokens), 0) == route, 1.0, 0.0)
    earlier = jnp.where(iota((tokens, tokens), 0) < iota((tokens, tokens), 1), 1.0, 0.0)
    before = jnp.dot(onehot.astype(BF), earlier.astype(BF), preferred_element_type=F32)
    return jnp.sum(before * onehot, axis=0, keepdims=True).astype(jnp.int32)


def main_onehot(route, slot, experts):
    place = jnp.where(slot < 8, route * 8 + slot, -1)
    return jnp.where(iota((experts * 8, route.shape[1]), 0) == place, 1.0, 0.0)


def tail_onehot(route, slot, experts, quarter):
    place = jnp.where(slot >= 8, route * 4 + quarter, -1)
    return jnp.where(iota((experts * 4, route.shape[1]), 0) == place, 1.0, 0.0)


def pack(route, experts, rows_of, send_ref):
    slot = slot_row(route, experts)
    main = main_onehot(route, slot, experts).astype(BF)
    planes = experts // 2
    tail = None
    for q in range(QUARTERS):
        rows = rows_of(q)
        width = rows.shape[1]
        sorted_rows = jnp.dot(main, rows, preferred_element_type=F32).reshape(planes, 2, 8, width)
        send_ref[:, q] = sorted_rows[:, 0].astype(BF)
        send_ref[:, 5 + q] = sorted_rows[:, 1].astype(BF)
        last = jnp.dot(
            tail_onehot(route, slot, experts, q).astype(BF), rows, preferred_element_type=F32
        )
        tail = last if tail is None else tail + last
    send_ref[:, 4] = tail.reshape(planes, 8, width).astype(BF)


def unpack(route, experts, back_ref):
    slot = slot_row(route, experts)
    main = main_onehot(route, slot, experts).T.astype(BF)
    planes = experts // 2
    width = back_ref.shape[3]

    def rows_of(q):
        first = back_ref[:, q].astype(F32)
        second = back_ref[:, 5 + q].astype(F32)
        both = jnp.stack([first, second], axis=1).reshape(experts * 8, width).astype(BF)
        last = back_ref[:, 4].astype(F32).reshape(planes * 8, width).astype(BF)
        tail = tail_onehot(route, slot, experts, q).T.astype(BF)
        return jnp.dot(main, both, preferred_element_type=F32) + jnp.dot(
            tail, last, preferred_element_type=F32
        )

    return rows_of


def quarter(q, width):
    return slice(q * width, (q + 1) * width)


def normed_rows(ref, gain_ref, width):
    tokens, features = ref.shape
    squares = jnp.zeros((tokens, 1), F32)
    for q in range(QUARTERS):
        part = ref[:, quarter(q, width)].astype(F32)
        squares += jnp.sum(part * part, axis=-1, keepdims=True)
    scale = lax.rsqrt(squares / features + EPS)

    def rows_of(q):
        cols = quarter(q, width)
        return (ref[:, cols].astype(F32) * scale * gain_ref[:, cols]).astype(BF)

    return rows_of


def as_column(row):
    count = row.shape[1]
    return jnp.broadcast_to(row, (count, count)).T[:, 0:1]


def attend(pair, first, sel_ref, query_ref, kv_ref, total):
    b, h = pair // KV_HEADS, pair % KV_HEADS
    keys = SEL * BLK
    blocks = query_ref.shape[0] // BLK
    token_rows = slice(b * BLK, (b + 1) * BLK)
    chosen = [sel_ref[b, h, k] for k in range(SEL)]
    held = [[], []]
    for k in range(SEL):
        owner = chosen[k] // blocks
        spot = (owner % 2, owner // (2 * NX), (owner // 2) % NX)
        for w in range(2):
            held[w].append(kv_ref[h][(*spot, w)])
    lane = iota((2 * BLK, keys), 1)
    key_pos = lane % BLK
    at, to = iota((blocks * BLK, keys), 0), iota((blocks * BLK, keys), 1)
    picks = []
    for k in range(SEL):
        key_pos = key_pos + jnp.where(lane // BLK == k, chosen[k] * BLK, 0)
        inside = (at == to % BLK + (chosen[k] % blocks) * BLK) & (to // BLK == k)
        picks.append(jnp.where(inside, 1.0, 0.0).astype(BF))
    allowed = key_pos <= (first + b) * BLK + iota((2 * BLK, keys), 0) % BLK

    def selected(pieces):
        out = None
        for piece, pick in zip(pieces, picks):
            more = jnp.dot(piece, pick, preferred_element_type=F32)
            out = more if out is None else out + more
        return out.astype(BF)

    key_cols, value_cols = selected(held[0]), selected(held[1])
    for g in range(GROUPS // 2):
        offset = (HEAD_DIM * g) % 128
        window = 128 if offset + HEAD_DIM <= 128 else 256
        shift = jnp.where(
            iota((window, HEAD_DIM), 0) == iota((window, HEAD_DIM), 1) + offset, 1.0, 0.0
        ).astype(BF)
        key_moved = jnp.dot(shift, key_cols, preferred_element_type=F32).astype(BF)
        value_moved = jnp.dot(shift, value_cols, preferred_element_type=F32).astype(BF)
        starts = [
            HEAD_DIM * (h * GROUPS + g + half * (GROUPS // 2)) // 128 * 128 for half in range(2)
        ]
        query = jnp.concatenate([query_ref[token_rows, s : s + window] for s in starts], axis=0)
        scores = jnp.dot(query, key_moved, preferred_element_type=F32) * HEAD_DIM ** (-0.5)
        scores = jnp.where(allowed, scores, NEG)
        exp_scores = jnp.exp(scores - jnp.max(scores, axis=-1, keepdims=True))
        weights = exp_scores / jnp.sum(exp_scores, axis=-1, keepdims=True)
        mixed = lax.dot_general(
            weights.astype(BF), value_moved, (((1,), (1,)), ((), ())), preferred_element_type=F32
        )
        for half, s in enumerate(starts):
            total[token_rows, s : s + window] += mixed[half * BLK : (half + 1) * BLK]

def tail_select(count, q):
    row, col = iota((count, count * 4), 0), iota((count, count * 4), 1)
    return jnp.where(col == row * 4 + q, 1.0, 0.0).astype(BF)


def rows_for_expert(main_ref, tail_ref, q):
    count, width = main_ref.shape[0], main_ref.shape[3]
    main = main_ref[:, q].astype(F32).reshape(count * 8, width).astype(BF)
    last = tail_ref[...].astype(F32).reshape(count * 4, width).astype(BF)
    tail = jnp.dot(tail_select(count, q), last, preferred_element_type=F32).astype(BF)
    return jnp.concatenate([main, tail], axis=0)


def store_for_source(main_ref, q, value, tail_total):
    count, width = main_ref.shape[0], main_ref.shape[3]
    main_ref[:, q] = value[: count * 8].reshape(count, 8, width).astype(BF)
    spread = lax.dot_general(
        tail_select(count, q), value[count * 8 :].astype(BF),
        (((0,), (0,)), ((), ())), preferred_element_type=F32,
    )
    return spread if tail_total is None else tail_total + spread


def forward_experts(recv, own, other, out):
    width = recv[0].shape[3]
    sides = (own, other)
    gates, ups = [None, None], [None, None]
    for q in range(QUARTERS):
        rows = rows_for_expert(*recv, q)
        part = quarter(q, width)
        for i, (g, u, _) in enumerate(sides):
            gate = jnp.dot(rows, g[part], preferred_element_type=F32)
            up = jnp.dot(rows, u[part], preferred_element_type=F32)
            gates[i] = gate if gates[i] is None else gates[i] + gate
            ups[i] = up if ups[i] is None else ups[i] + up
    hidden = [(v / (1.0 + jnp.exp(-v)) * u).astype(BF) for v, u in zip(gates, ups)]
    tail = None
    for q in range(QUARTERS):
        part = quarter(q, width)
        value = jnp.dot(hidden[0], own[2][:, part], preferred_element_type=F32) + jnp.dot(
            hidden[1], other[2][:, part], preferred_element_type=F32
        )
        tail = store_for_source(out[0], q, value, tail)
    out[1][...] = tail.reshape(out[1].shape).astype(BF)


def backward_experts(recv, recv_grad, own, other, out):
    width = recv[0].shape[3]
    last = (((1,), (1,)), ((), ()))
    sides = (own, other)
    gates, ups, downs = [None, None], [None, None], [None, None]
    for q in range(QUARTERS):
        rows = rows_for_expert(*recv, q)
        grads = rows_for_expert(*recv_grad, q)
        part = quarter(q, width)
        for i, (g, u, d) in enumerate(sides):
            gate = jnp.dot(rows, g[part], preferred_element_type=F32)
            up = jnp.dot(rows, u[part], preferred_element_type=F32)
            down = lax.dot_general(grads, d[:, part], last, preferred_element_type=F32)
            gates[i] = gate if gates[i] is None else gates[i] + gate
            ups[i] = up if ups[i] is None else ups[i] + up
            downs[i] = down if downs[i] is None else downs[i] + down
    gate_grads, up_grads = [], []
    for gate, up, down in zip(gates, ups, downs):
        sigmoid = 1.0 / (1.0 + jnp.exp(-gate))
        gate_grads.append((down * up * (sigmoid * (1.0 + gate * (1.0 - sigmoid)))).astype(BF))
        up_grads.append((down * (gate * sigmoid)).astype(BF))
    tail = None
    for q in range(QUARTERS):
        part = quarter(q, width)
        value = None
        for i, (g, u, _) in enumerate(sides):
            more = lax.dot_general(
                gate_grads[i], g[part], last, preferred_element_type=F32
            ) + lax.dot_general(up_grads[i], u[part], last, preferred_element_type=F32)
            value = more if value is None else value + more
        tail = store_for_source(out[0], q, value, tail)
    out[1][...] = tail.reshape(out[1].shape).astype(BF)


def front_last_kernel(
    middle_hbm, back_hbm, meta_hbm, done_hbm, out_hbm, done_out,
    middle_ref, back_ref, meta_ref, out_ref, done_ref, sem,
):
    width = back_ref.shape[3]
    experts = back_ref.shape[0] * 2
    pairs = (
        (meta_hbm, meta_ref), (back_hbm, back_ref), (middle_hbm, middle_ref), (done_hbm, done_ref),
    )
    copies = [pltpu.make_async_copy(a, b, sem.at[i]) for i, (a, b) in enumerate(pairs)]
    for copy in copies:
        copy.start()
    for copy in copies:
        copy.wait()
    copies = [pltpu.make_async_copy(done_ref, done_out, sem.at[4])]
    copies[0].start()
    gate = as_column(meta_ref[0:1])
    rows_of = unpack(meta_ref[1:2].astype(jnp.int32), experts, back_ref)
    for q in range(QUARTERS):
        cols = quarter(q, width)
        out_ref[:, cols] = (middle_ref[:, cols].astype(F32) + gate * rows_of(q)).astype(BF)
        copy = pltpu.make_async_copy(out_ref.at[:, cols], out_hbm.at[:, cols], sem.at[5 + q])
        copy.start()
        copies.append(copy)
    for copy in copies:
        copy.wait()


def back_last(mid_ref, grad_ref, gain_ref, back_ref, meta_ref, out_ref, amount):
    experts = back_ref.shape[0] * 2
    width = back_ref.shape[3]
    tokens, features = mid_ref.shape
    rows_of = unpack(meta_ref[1:2].astype(jnp.int32), experts, back_ref)
    squares = jnp.zeros((tokens, 1), F32)
    products = jnp.zeros((tokens, 1), F32)
    for q in range(QUARTERS):
        cols = quarter(q, width)
        mid = mid_ref[:, cols].astype(F32)
        value = gain_ref[:, cols] * rows_of(q)
        amount[:, cols] = value
        squares += jnp.sum(mid * mid, axis=-1, keepdims=True)
        products += jnp.sum(mid * value, axis=-1, keepdims=True)
    scale = lax.rsqrt(squares / features + EPS)
    factor = scale * scale * scale * (products / features)
    for q in range(QUARTERS):
        cols = quarter(q, width)
        out_ref[:, cols] = (
            grad_ref[:, cols].astype(F32)
            + scale * amount[:, cols]
            - mid_ref[:, cols].astype(F32) * factor
        ).astype(BF)


def place():
    section, index = lax.axis_index("section"), lax.axis_index("expert")
    return section, index // (2 * NX), (index // 2) % NX, index % 2


def device(section, z, x, core):
    return (section, (z * NX + x) * 2 + core)


def far_first(planes):
    return sorted(range(1, planes), key=lambda d: -min(d, planes - d))


def stages_of(planes):
    return [sorted({d, planes - d}) for d in range(1, planes // 2 + 1)]


class Flow:
    def __init__(self, items, depth):
        self.unsent = list(items)
        self.waiting = []
        self.depth = depth

    def fill(self):
        while self.unsent and self.sent < self.depth:
            one, d = self.unsent.pop(0)
            one.send(d)
            self.waiting.append((one, d))
            self.sent += 1

    def open(self):
        self.sent = 0
        self.fill()

    def more(self, items):
        self.unsent += items
        self.fill()

    def left(self):
        return len(self.waiting) + len(self.unsent)

    def turn(self, count=1):
        for _ in range(count):
            one, d = self.waiting.pop(0)
            self.sent -= 1
            self.fill()
            one.forward(d)


def greet(targets):
    barrier = pltpu.get_barrier_semaphore()
    for target in targets:
        pl.semaphore_signal(barrier, inc=1, device_id=target, device_id_type=MESH)
    pl.semaphore_wait(barrier, len(targets))


def remote(src, dst, send, recv, target):
    return pltpu.make_async_remote_copy(
        src_ref=src, dst_ref=dst, send_sem=send, recv_sem=recv,
        device_id=target, device_id_type=MESH,
    )


def dma(*shape):
    return pltpu.SemaphoreType.DMA(shape)


class Gather:
    def __init__(self, kv, zsend, zrecv, xsend, xrecv, csend, crecv):
        self.kv = kv
        self.sems = (zsend, zrecv, xsend, xrecv, csend, crecv)
        self.planes = kv[0].shape[1]
        self.started = []

    def go(self, ref, send, recv, target):
        copy = remote(ref, ref, send, recv, target)
        copy.start()
        self.started.append(copy)

    def along_x(self, h, origin, d):
        _, _, xsend, xrecv, _, _ = self.sems
        s, z, x, c = place()
        for dx in (2, 1, 3):
            self.go(
                self.kv[h].at[c, origin, x], xsend.at[h, d, dx - 1], xrecv.at[h, origin, x],
                device(s, z, (x + dx) % NX, c),
            )

    def await_x(self, h, origin, d):
        _, _, xsend, xrecv, _, _ = self.sems
        s, z, x, c = place()
        for dx in (1, 3, 2):
            ref = self.kv[h].at[c, origin, (x + dx) % NX]
            remote(
                ref, ref, xsend.at[h, d, dx - 1], xrecv.at[h, origin, (x + dx) % NX],
                device(s, z, (x + dx) % NX, c),
            ).wait_recv()

    def z_ref(self, h, origin):
        _, _, x, c = place()
        return self.kv[0].at[c, origin, x] if h == 0 else self.kv[1].at[c, origin]

    def along_z(self, h, d, way):
        zsend, zrecv = self.sems[:2]
        s, z, x, c = place()
        origin = (z - way * d + self.planes) % self.planes
        self.go(
            self.z_ref(h, origin), zsend.at[h, (way + 1) // 2, d], zrecv.at[h, origin],
            device(s, (z + way + self.planes) % self.planes, x, c),
        )

    def await_z(self, h, d, way):
        zsend, zrecv = self.sems[:2]
        s, z, x, c = place()
        origin = (z - way * d + self.planes) % self.planes
        ref = self.z_ref(h, origin)
        remote(
            ref, ref, zsend.at[h, (way + 1) // 2, d], zrecv.at[h, origin], device(s, origin, x, c)
        ).wait_recv()
        return origin

    def swap(self, h, origin):
        _, _, _, _, csend, crecv = self.sems
        s, z, x, c = place()
        self.go(
            self.kv[h].at[c, origin], csend.at[h, origin], crecv.at[h, origin],
            device(s, z, x, 1 - c),
        )

    def reach(self, way):
        return self.planes // 2 if way == 1 else (self.planes - 1) // 2

    def start(self):
        _, z, x, c = place()
        self.along_x(1, z, 0)
        for way in (1, -1):
            if self.reach(way) > 0:
                self.along_z(0, 0, way)
        self.along_x(0, z, 0)

    def turn(self):
        z = place()[1]
        self.await_x(1, z, 0)
        for way in (1, -1):
            if self.reach(way) > 0:
                self.along_z(1, 0, way)
        self.swap(1, z)

    def step(self, d):
        for h in (0, 1):
            for way in (1, -1):
                if d <= self.reach(way):
                    origin = self.await_z(h, d, way)
                    if d < self.reach(way):
                        self.along_z(h, d, way)
                    if h == 0:
                        self.along_x(0, origin, d if way == 1 else self.planes - d)
                    else:
                        self.swap(1, origin)

    def settle(self):
        z = place()[1]
        for d in range(self.planes // 2 + 1):
            for way in (1, -1):
                if d <= self.reach(way) and (d > 0 or way == 1):
                    origin = (z - way * d + self.planes) % self.planes
                    self.await_x(0, origin, d if way == 1 else self.planes - d)
                    self.swap(0, origin)

    def ready(self, h):
        _, _, _, _, csend, crecv = self.sems
        s, z, x, c = place()
        for k in range(self.planes):
            ref = self.kv[h].at[1 - c, k]
            remote(ref, ref, csend.at[h, k], crecv.at[h, k], device(s, z, x, 1 - c)).wait_recv()

    def drain(self):
        for copy in self.started:
            copy.wait_send()

    @staticmethod
    def scratch(planes):
        return [
            dma(2, 2, planes), dma(2, planes), dma(2, planes, NX - 1), dma(2, planes, NX),
            dma(2, planes), dma(2, planes),
        ]


def join(first, second, half):
    upper = iota(first.shape, 0) < 4
    if half == 0:
        return jnp.where(upper, first, pltpu.roll(second, 4, 0))
    return jnp.where(upper, pltpu.roll(first, 4, 0), second)


class Dispatch:
    def __init__(
        self, send_ref, zbuf, shared, main, tail, zsend, zrecv, xsend, xrecv, tsend, trecv, local
    ):
        self.refs = (send_ref, zbuf, shared, main, tail)
        self.sems = (zsend, zrecv, xsend, xrecv, tsend, trecv, local)
        self.planes = send_ref.shape[0]
        self.started = []
        self.local = []

    def send(self, d):
        send_ref, zbuf = self.refs[:2]
        zsend, zrecv = self.sems[:2]
        s, z, x, c = place()
        to = (z + d) % self.planes
        copy = remote(
            send_ref.at[to], zbuf.at[z], zsend.at[d], zrecv.at[z], device(s, to, x, c)
        )
        copy.start()
        self.started.append(copy)

    def send_stages(self, stages):
        for stage in stages:
            for d in stage:
                self.send(d)

    def forward_all(self, k):
        stages = stages_of(self.planes)
        for d in stages[k]:
            self.forward(d)
        for j in {0: (0,), 2: (1, 3), 3: (2,)}.get(k, ()):
            self.forward_tail(j)

    def forward(self, d):
        send_ref, zbuf, _, main, _ = self.refs
        zsend, zrecv, xsend, xrecv, _, _, local = self.sems
        s, z, x, c = place()
        origin = (z + d) % self.planes
        source = zbuf.at[origin]
        if d == 0:
            source = send_ref.at[z]
            zbuf[z, 4] = send_ref[z, 4]
        else:
            remote(
                send_ref.at[origin], zbuf.at[origin], zsend.at[d], zrecv.at[origin],
                device(s, origin, x, c),
            ).wait_recv()
        for dx in (2, 1, 3):
            to = (x + dx) % NX
            copy = remote(
                source.at[pl.ds(5 * (to // 2), 4)], main.at[x * self.planes + origin],
                xsend.at[dx - 1, d], xrecv.at[x, origin], device(s, z, to, c),
            )
            copy.start()
            self.started.append(copy)
        mine = pltpu.make_async_copy(
            source.at[pl.ds(5 * (x // 2), 4)], main.at[x * self.planes + origin], local.at[d]
        )
        mine.start()
        self.local.append(mine)

    def pair(self, j):
        half = self.planes // 2
        return (place()[1] // 2 + j) % half

    def forward_tail(self, j):
        _, zbuf, shared, _, tail = self.refs
        _, _, _, _, tsend, trecv, _ = self.sems
        s, z, x, c = place()
        half = self.planes // 2
        p = self.pair(j)
        first, second = zbuf[2 * p, 4].astype(F32), zbuf[2 * p + 1, 4].astype(F32)
        for h in range(2):
            shared[p, h] = join(first, second, h).astype(BF)
        for dx in (2, 1, 3):
            to = (x + dx) % NX
            copy = remote(
                shared.at[p, to // 2], tail.at[x * half + p], tsend.at[dx - 1, j],
                trecv.at[x, p], device(s, z, to, c),
            )
            copy.start()
            self.started.append(copy)
        tail[x * half + p] = shared[p, x // 2]

    def arrive(self):
        send_ref, zbuf, shared, main, tail = self.refs
        zsend, zrecv, xsend, xrecv, tsend, trecv, local = self.sems
        s, z, x, c = place()
        half = self.planes // 2
        for d in range(self.planes):
            origin = (z + d) % self.planes
            for dx in range(1, NX):
                source = (x + dx) % NX
                remote(
                    zbuf.at[origin, pl.ds(0, 4)], main.at[source * self.planes + origin],
                    xsend.at[dx - 1, d], xrecv.at[source, origin], device(s, z, source, c),
                ).wait_recv()
        for j in range(half):
            p = self.pair(j)
            for dx in range(1, NX):
                source = (x + dx) % NX
                remote(
                    shared.at[p, 0], tail.at[source * half + p], tsend.at[dx - 1, j],
                    trecv.at[source, p], device(s, z, source, c),
                ).wait_recv()
        for copy in self.local:
            copy.wait()

    def drain(self):
        for copy in self.started:
            copy.wait_send()

    @staticmethod
    def scratch(planes):
        half = planes // 2
        return [
            dma(planes), dma(planes), dma(NX - 1, planes), dma(NX, planes),
            dma(NX - 1, half), dma(NX, half), dma(planes),
        ]


class Return:
    def __init__(
        self, main, tail, pmain, ptail, stage, out_ref, by, xsend, xrecv, tsend, trecv, zsend, zrecv
    ):
        self.refs = (main, tail, pmain, ptail, stage, out_ref)
        self.sems = (xsend, xrecv, tsend, trecv, zsend, zrecv)
        self.planes = stage.shape[0]
        self.by = by
        self.started = []

    def order(self):
        half = self.planes // 2
        return sorted(range(half), key=lambda j: -min(j, half - j))

    def pair(self, j):
        half = self.planes // 2
        return (place()[1] // 2 + j) % half

    def messages(self, j, mine):
        main, tail, pmain, ptail, _, _ = self.refs
        xsend, xrecv, tsend, trecv, _, _ = self.sems
        half = self.planes // 2
        p = self.pair(j)
        for dx in (2, 1, 3):
            other = (place()[2] + dx) % NX
            left = other if mine else place()[2]
            spot = place()[2] if mine else other
            for k in range(2):
                origin = 2 * p + k
                yield (
                    main.at[left * self.planes + origin], pmain.at[spot * self.planes + origin],
                    xsend.at[dx - 1, 2 * j + k], xrecv.at[spot, origin], other,
                )
            yield (
                tail.at[left * half + p], ptail.at[spot * half + p],
                tsend.at[dx - 1, j], trecv.at[spot, p], other,
            )

    def send(self, j):
        s, z, x, c = place()
        for source, target, sent, came, other in self.messages(j, True):
            copy = remote(source, target, sent, came, device(s, z, other, c))
            copy.start()
            self.started.append(copy)

    def forward(self, j):
        main, tail, pmain, ptail, stage, out_ref = self.refs
        _, _, _, _, zsend, zrecv = self.sems
        s, z, x, c = place()
        half = self.planes // 2
        p = self.pair(j)
        for k in range(2):
            mine = x * self.planes + 2 * p + k
            pmain[mine] = main[mine]
        ptail[x * half + p] = tail[x * half + p]
        for source, target, sent, came, other in self.messages(j, False):
            remote(source, target, sent, came, device(s, z, other, c)).wait_recv()

        def last(source):
            return ptail[source * half + p].astype(F32)

        first, second = last(0) + last(1), last(2) + last(3)
        sections = lax.axis_size("section")
        for k in range(2):
            origin = 2 * p + k

            def piece(source, q):
                return pmain[source * self.planes + origin, q].astype(F32)

            for q in range(QUARTERS):
                stage[origin, q] = (piece(0, q) + piece(1, q)).astype(BF)
                stage[origin, 5 + q] = (piece(2, q) + piece(3, q)).astype(BF)
            stage[origin, 4] = join(first, second, k).astype(BF)
            copy = remote(
                stage.at[origin], out_ref.at[z], zsend.at[2 * j + k], zrecv.at[z],
                device((s + self.by + sections) % sections, origin, x, c),
            )
            copy.start()
            self.started.append(copy)

    def arrive(self):
        stage, out_ref = self.refs[4:]
        zsend, zrecv = self.sems[4:]
        s, z, x, c = place()
        sections = lax.axis_size("section")
        for d in range(self.planes):
            origin = (z + d) % self.planes
            remote(
                stage.at[origin], out_ref.at[origin], zsend.at[d], zrecv.at[origin],
                device((s - self.by + sections) % sections, origin, x, c),
            ).wait_recv()

    def drain(self):
        for copy in self.started:
            copy.wait_send()

    @staticmethod
    def scratch(planes):
        half = planes // 2
        return [
            dma(NX - 1, planes), dma(NX, planes), dma(NX - 1, half), dma(NX, half),
            dma(planes), dma(planes),
        ]


def everyone(planes, sections):
    s, z, x, c = place()
    peers = [device(s, (z + d) % planes, x, c) for d in range(1, planes)]
    peers += [device(s, z, (x + d) % NX, c) for d in range(1, NX)]
    peers += [
        device((s + by) % sections, (z + d) % planes, x, c)
        for by in (1, sections - 1) for d in range(planes)
    ]
    return peers + [device(s, z, x, 1 - c)]


def hand_over(refs, outs, send, recv, target):
    copies = []
    for i, (ref, out) in enumerate(zip(refs, outs)):
        copy = remote(ref, out, send.at[i], recv.at[i], target)
        copy.start()
        copies.append(copy)
    return copies


NAMES = (
    "mid", "grad", "query", "entry", "own_g", "own_u", "own_d", "other_g", "other_u", "other_d",
    "kv0", "kv1", "total", "middle", "rows0", "rows1", "rows2", "zbuf0", "zbuf1", "zbuf2", "recv0",
    "recv1", "recv2", "part0", "part1", "pbuf0", "pbuf1", "stage0", "stage1", "back_in",
    "last0", "last1", "last2", "plast0", "plast1", "blast0", "blast1",
    "shared0", "shared1", "shared2",
    "mid_in", "grad_in", "gain_in", "b_meta", "f_meta", "b_meta_in", "result",
)


def main_kernel(
    sel, kv_in, gain, f_route, f_gate, b_route, b_gate,
    mid_hbm, grad_hbm, query_hbm, entry_hbm, wg, wu, wd,
    result_out, middle_out, f_meta_out, front_out,
    *scratch,
):
    v = dict(zip(NAMES, scratch))
    sems = list(scratch[len(NAMES) :])
    s, z, x, c = place()
    sections = lax.axis_size("section")
    planes = v["rows0"].shape[0]
    width = v["rows0"].shape[3]
    experts = planes * 2
    load, csend, crecv, ysend, yrecv = sems[:5]
    sems = sems[5:]
    kv = (v["kv0"], v["kv1"])
    gather = Gather(kv, *sems[:6])
    sends = [
        Dispatch(
            v[f"rows{i}"], v[f"zbuf{i}"], v[f"shared{i}"], v[f"recv{i}"], v[f"last{i}"],
            *sems[6 + 7 * i : 13 + 7 * i],
        )
        for i in range(3)
    ]
    ones, twos, front = sends
    back_ret, front_ret = [
        Return(
            v[f"part{i}"], v[f"plast{i}"], v[f"pbuf{i}"], v[f"blast{i}"], v[f"stage{i}"],
            (v["back_in"], front_out)[i], (-1, 1)[i], *sems[27 + 6 * i : 33 + 6 * i],
        )
        for i in range(2)
    ]

    local = []
    for i, (source, name) in enumerate(
        zip(
            (mid_hbm, grad_hbm, query_hbm, entry_hbm, wg, wu, wd),
            ("mid", "grad", "query", "entry", "own_g", "own_u", "own_d"),
        )
    ):
        copy = pltpu.make_async_copy(source, v[name], load.at[i])
        copy.start()
        local.append(copy)
    for head in range(KV_HEADS):
        for w in range(2):
            kv[head][c, z, x, w] = kv_in[w * KV_HEADS + head]
    for name, gate_ref, route_ref in (("b_meta", b_gate, b_route), ("f_meta", f_gate, f_route)):
        v[name][...] = jnp.zeros_like(v[name])
        v[name][0:1] = gate_ref[...]
        v[name][1:2] = route_ref[...].astype(F32)
    v["total"][...] = jnp.zeros_like(v["total"])
    greet(everyone(planes, sections))
    stages = stages_of(planes)
    gather.start()
    local[0].wait()
    pack(b_route[...], experts, normed_rows(v["mid"], gain, width), v["rows0"])
    ones.send_stages(stages[:2])
    ones.forward(0)
    gather.turn()
    gate = as_column(b_gate[...])
    local[1].wait()

    def scaled(q):
        return (gate * v["grad"][:, quarter(q, width)].astype(F32)).astype(BF)

    pack(b_route[...], experts, scaled, v["rows1"])
    twos.forward(0)
    before = device((s + sections - 1) % sections, z, x, c)
    after = device((s + 1) % sections, z, x, c)
    shipped = hand_over(
        (v["mid"], v["grad"], gain, v["b_meta"]),
        (v["mid_in"], v["grad_in"], v["gain_in"], v["b_meta_in"]),
        ysend.at[0], yrecv.at[0], before,
    )
    gather.step(1)
    ones.forward_all(0)
    ones.send_stages(stages[2:3])
    ones.forward_all(1)
    gather.step(2)
    ones.send_stages(stages[3:4])
    twos.send_stages(stages[0:1])
    ones.forward_all(2)
    gather.step(3)
    twos.send_stages(stages[1:3])
    ones.forward_all(3)
    twos.forward_all(0)
    gather.step(4)
    twos.send_stages(stages[3:4])
    twos.forward_all(1)
    gather.settle()
    weights = hand_over(
        (wg, wu, wd), (v["other_g"], v["other_u"], v["other_d"]), csend, crecv,
        device(s, z, x, 1 - c),
    )
    for copy in local[2:4]:
        copy.wait()
    blocks = v["query"].shape[0] // BLK
    first = lax.axis_index("expert") * blocks
    for head in (1, 0):
        gather.ready(head)
        for b in range(blocks):
            attend(b * KV_HEADS + head, first, sel, v["query"], kv, v["total"])
        if head == 1:
            twos.forward_all(2)
    for q in range(QUARTERS):
        cols = quarter(q, width)
        v["middle"][:, cols] = (
            v["entry"][:, cols].astype(F32) + v["total"][:, cols]
        ).astype(BF)
    pack(f_route[...], experts, normed_rows(v["middle"], gain, width), v["rows2"])
    front.send_stages(stages)
    front.forward(0)
    twos.forward_all(3)
    shipped += hand_over(
        (v["middle"], v["f_meta"]), (middle_out, f_meta_out), ysend.at[1], yrecv.at[1], after
    )
    front.forward_all(0)
    ones.arrive()
    twos.arrive()
    for copy in local[4:]:
        copy.wait()
    for copy in weights:
        copy.wait()
    own = (v["own_g"], v["own_u"], v["own_d"])
    other = (v["other_g"], v["other_u"], v["other_d"])
    backward_experts(
        (v["recv0"], v["last0"]), (v["recv1"], v["last1"]), own, other, (v["part0"], v["plast0"])
    )
    turns = back_ret.order()
    flow = Flow([(back_ret, d) for d in turns], 2)
    flow.open()
    front.forward_all(1)
    front.forward_all(2)
    flow.turn()
    front.forward_all(3)
    flow.turn()
    front.arrive()
    forward_experts((v["recv2"], v["last2"]), own, other, (v["part1"], v["plast1"]))
    flow.more([(front_ret, d) for d in turns])
    flow.turn(flow.left() - len(turns) // 2)
    back_ret.arrive()
    for copy in shipped:
        copy.wait()
    back_last(
        v["mid_in"], v["grad_in"], v["gain_in"], v["back_in"], v["b_meta_in"],
        v["result"], v["total"],
    )
    last = pltpu.make_async_copy(v["result"], result_out, load.at[7])
    last.start()
    flow.turn(flow.left())
    front_ret.arrive()
    last.wait()
    for one in (gather, ones, twos, front, back_ret, front_ret):
        one.drain()


ANY = pl.BlockSpec(memory_space=pl.ANY)
VMEM = pl.BlockSpec(memory_space=pltpu.VMEM)
SMEM = pl.BlockSpec(memory_space=pltpu.SMEM)


def shards(
    front_input, queries, keys_values, selected_blocks, front_route, front_gate,
    back_middle, back_grad, back_route, back_gate, norm_gain, gate_slice, up_slice, down_slice,
):
    tokens, features = front_input.shape[1:]
    planes = lax.axis_size("expert") // (2 * NX)
    width = features // QUARTERS
    kv = keys_values[0].T.reshape(2 * KV_HEADS, HEAD_DIM, tokens)
    message = pltpu.VMEM((planes, 9, 8, width), BF)
    arrived = pltpu.VMEM((NX * planes, QUARTERS, 8, width), BF)
    lasts = pltpu.VMEM((NX * planes // 2, 8, width), BF)
    rows = pltpu.VMEM((tokens, features), BF)
    tall = pltpu.VMEM(gate_slice.shape[2:], BF)
    flat = pltpu.VMEM(down_slice.shape[2:], BF)
    meta = pltpu.VMEM((8, tokens), F32)
    half_kv = pltpu.VMEM((2, planes, NX, 2, HEAD_DIM, tokens), BF)
    shapes = dict(
        mid=rows, grad=rows, query=rows, entry=rows, own_g=tall, own_u=tall, own_d=flat,
        other_g=tall, other_u=tall, other_d=flat,
        kv0=half_kv, kv1=half_kv,
        total=pltpu.VMEM((tokens, features), F32), middle=rows,
        back_in=message, mid_in=rows, grad_in=rows, gain_in=pltpu.VMEM((1, features), F32),
        b_meta=meta, f_meta=meta, b_meta_in=meta, result=rows,
    )
    for i in range(3):
        shapes[f"rows{i}"] = shapes[f"zbuf{i}"] = message
        shapes[f"recv{i}"] = shapes[f"part{i}"] = shapes[f"pbuf{i}"] = arrived
        shapes[f"stage{i}"] = message
        shapes[f"last{i}"] = shapes[f"plast{i}"] = shapes[f"blast{i}"] = lasts
        shapes[f"shared{i}"] = pltpu.VMEM((planes // 2, 2, 8, width), BF)
    result, middle, f_meta, front = pl.pallas_call(
        main_kernel,
        out_shape=[
            jax.ShapeDtypeStruct((tokens, features), BF),
            jax.ShapeDtypeStruct((tokens, features), BF),
            jax.ShapeDtypeStruct((8, tokens), F32),
            jax.ShapeDtypeStruct((planes, 9, 8, width), BF),
        ],
        in_specs=[SMEM] + [VMEM] * 6 + [ANY] * 7,
        out_specs=[ANY] * 4,
        scratch_shapes=[shapes[name] for name in NAMES]
        + [dma(8), dma(3), dma(3), dma(2, 4), dma(2, 4)]
        + Gather.scratch(planes) + Dispatch.scratch(planes) * 3 + Return.scratch(planes) * 2,
        compiler_params=pltpu.CompilerParams(
            collective_id=0, has_side_effects=True, vmem_limit_bytes=63 << 20
        ),
        name="layer",
    )(
        selected_blocks[0], kv, norm_gain,
        front_route.reshape(1, tokens), front_gate.reshape(1, tokens),
        back_route.reshape(1, tokens), back_gate.reshape(1, tokens),
        back_middle[0], back_grad[0], queries[0], front_input[0],
        gate_slice[0, 0], up_slice[0, 0], down_slice[0, 0],
    )
    front_output, back_output = pl.pallas_call(
        front_last_kernel,
        out_shape=[jax.ShapeDtypeStruct((tokens, features), BF)] * 2,
        in_specs=[ANY] * 4,
        out_specs=[ANY] * 2,
        scratch_shapes=[rows, message, meta, rows, rows, dma(5 + QUARTERS)],
        compiler_params=pltpu.CompilerParams(vmem_limit_bytes=63 << 20),
        name="front_last",
    )(middle, front, f_meta, result)
    return (front_output[None], back_output[None])


def solution(mesh):
    rows = P("section", "expert", None)
    wide = P("section", "expert", None, None)
    return jax.shard_map(
        shards,
        mesh=mesh,
        in_specs=(rows, rows, rows, wide, rows, rows, rows, rows, rows, rows,
                  P("section", None), wide, wide, wide),
        out_specs=(rows, rows),
        check_vma=False,
    )
```

```python
import jax
import jax.numpy as jnp
from jax import lax
from jax.experimental import pallas as pl
from jax.experimental.pallas import tpu as pltpu
from jax.sharding import PartitionSpec as P

HEADS = 32
HEAD_DIM = 112
KV_HEADS = 2
GROUPS = HEADS // KV_HEADS
BLK = 64
SEL = 4
QUARTERS = 4
NX = 4
EPS = 1e-06
NEG = -1e30
MESH = pl.DeviceIdType.MESH
BF = jnp.bfloat16
F32 = jnp.float32


def iota(shape, dim):
    return lax.broadcasted_iota(jnp.int32, shape, dim)


def slot_row(route, experts):
    tokens = route.shape[1]
    onehot = jnp.where(iota((experts, tokens), 0) == route, 1.0, 0.0)
    earlier = jnp.where(iota((tokens, tokens), 0) < iota((tokens, tokens), 1), 1.0, 0.0)
    before = jnp.dot(onehot.astype(BF), earlier.astype(BF), preferred_element_type=F32)
    return jnp.sum(before * onehot, axis=0, keepdims=True).astype(jnp.int32)


def main_onehot(route, slot, experts):
    place = jnp.where(slot < 8, route * 8 + slot, -1)
    return jnp.where(iota((experts * 8, route.shape[1]), 0) == place, 1.0, 0.0)


def tail_onehot(route, slot, experts, quarter):
    place = jnp.where(slot >= 8, route * 4 + quarter, -1)
    return jnp.where(iota((experts * 4, route.shape[1]), 0) == place, 1.0, 0.0)


def pack(route, experts, rows_of, send_ref):
    slot = slot_row(route, experts)
    main = main_onehot(route, slot, experts).astype(BF)
    planes = experts // 2
    tail = None
    for q in range(QUARTERS):
        rows = rows_of(q)
        width = rows.shape[1]
        sorted_rows = jnp.dot(main, rows, preferred_element_type=F32).reshape(planes, 2, 8, width)
        send_ref[:, q] = sorted_rows[:, 0].astype(BF)
        send_ref[:, 5 + q] = sorted_rows[:, 1].astype(BF)
        last = jnp.dot(
            tail_onehot(route, slot, experts, q).astype(BF), rows, preferred_element_type=F32
        )
        tail = last if tail is None else tail + last
    send_ref[:, 4] = tail.reshape(planes, 8, width).astype(BF)


def unpack(route, experts, back_ref):
    slot = slot_row(route, experts)
    main = main_onehot(route, slot, experts).T.astype(BF)
    planes = experts // 2
    width = back_ref.shape[3]

    def rows_of(q):
        first = back_ref[:, q].astype(F32)
        second = back_ref[:, 5 + q].astype(F32)
        both = jnp.stack([first, second], axis=1).reshape(experts * 8, width).astype(BF)
        last = back_ref[:, 4].astype(F32).reshape(planes * 8, width).astype(BF)
        tail = tail_onehot(route, slot, experts, q).T.astype(BF)
        return jnp.dot(main, both, preferred_element_type=F32) + jnp.dot(
            tail, last, preferred_element_type=F32
        )

    return rows_of


def quarter(q, width):
    return slice(q * width, (q + 1) * width)


def normed_rows(ref, gain_ref, width):
    tokens, features = ref.shape
    squares = jnp.zeros((tokens, 1), F32)
    for q in range(QUARTERS):
        part = ref[:, quarter(q, width)].astype(F32)
        squares += jnp.sum(part * part, axis=-1, keepdims=True)
    scale = lax.rsqrt(squares / features + EPS)

    def rows_of(q):
        cols = quarter(q, width)
        return (ref[:, cols].astype(F32) * scale * gain_ref[:, cols]).astype(BF)

    return rows_of


def as_column(row):
    count = row.shape[1]
    return jnp.broadcast_to(row, (count, count)).T[:, 0:1]


def attend(pair, first, sel_ref, query_ref, kv_ref, total):
    b, h = pair // KV_HEADS, pair % KV_HEADS
    keys = SEL * BLK
    blocks = query_ref.shape[0] // BLK
    token_rows = slice(b * BLK, (b + 1) * BLK)
    chosen = [sel_ref[b, h, k] for k in range(SEL)]
    held = [[], []]
    for k in range(SEL):
        owner = chosen[k] // blocks
        spot = (owner % 2, owner // (2 * NX), (owner // 2) % NX)
        for w in range(2):
            held[w].append(kv_ref[h][(*spot, w)])
    lane = iota((2 * BLK, keys), 1)
    key_pos = lane % BLK
    at, to = iota((blocks * BLK, keys), 0), iota((blocks * BLK, keys), 1)
    picks = []
    for k in range(SEL):
        key_pos = key_pos + jnp.where(lane // BLK == k, chosen[k] * BLK, 0)
        inside = (at == to % BLK + (chosen[k] % blocks) * BLK) & (to // BLK == k)
        picks.append(jnp.where(inside, 1.0, 0.0).astype(BF))
    allowed = key_pos <= (first + b) * BLK + iota((2 * BLK, keys), 0) % BLK

    def selected(pieces):
        out = None
        for piece, pick in zip(pieces, picks):
            more = jnp.dot(piece, pick, preferred_element_type=F32)
            out = more if out is None else out + more
        return out.astype(BF)

    key_cols, value_cols = selected(held[0]), selected(held[1])
    for g in range(GROUPS // 2):
        offset = (HEAD_DIM * g) % 128
        window = 128 if offset + HEAD_DIM <= 128 else 256
        shift = jnp.where(
            iota((window, HEAD_DIM), 0) == iota((window, HEAD_DIM), 1) + offset, 1.0, 0.0
        ).astype(BF)
        key_moved = jnp.dot(shift, key_cols, preferred_element_type=F32).astype(BF)
        value_moved = jnp.dot(shift, value_cols, preferred_element_type=F32).astype(BF)
        starts = [
            HEAD_DIM * (h * GROUPS + g + half * (GROUPS // 2)) // 128 * 128 for half in range(2)
        ]
        query = jnp.concatenate([query_ref[token_rows, s : s + window] for s in starts], axis=0)
        scores = jnp.dot(query, key_moved, preferred_element_type=F32) * HEAD_DIM ** (-0.5)
        scores = jnp.where(allowed, scores, NEG)
        exp_scores = jnp.exp(scores - jnp.max(scores, axis=-1, keepdims=True))
        weights = exp_scores / jnp.sum(exp_scores, axis=-1, keepdims=True)
        mixed = lax.dot_general(
            weights.astype(BF), value_moved, (((1,), (1,)), ((), ())), preferred_element_type=F32
        )
        for half, s in enumerate(starts):
            total[token_rows, s : s + window] += mixed[half * BLK : (half + 1) * BLK]

def tail_select(count, q):
    row, col = iota((count, count * 4), 0), iota((count, count * 4), 1)
    return jnp.where(col == row * 4 + q, 1.0, 0.0).astype(BF)


def gather_rows(recv, rows_ref):
    main_ref, tail_ref = recv
    count, width = main_ref.shape[0], main_ref.shape[3]
    last = tail_ref[...].astype(F32).reshape(count * 4, width).astype(BF)
    for q in range(QUARTERS):
        cols = quarter(q, width)
        rows_ref[: count * 8, cols] = (
            main_ref[:, q].astype(F32).reshape(count * 8, width).astype(BF)
        )
        rows_ref[count * 8 :, cols] = jnp.dot(
            tail_select(count, q), last, preferred_element_type=F32
        ).astype(BF)


def store_for_source(main_ref, q, value, tail_total):
    count, width = main_ref.shape[0], main_ref.shape[3]
    main_ref[:, q] = value[: count * 8].reshape(count, 8, width).astype(BF)
    spread = lax.dot_general(
        tail_select(count, q), value[count * 8 :].astype(BF),
        (((0,), (0,)), ((), ())), preferred_element_type=F32,
    )
    return spread if tail_total is None else tail_total + spread


def forward_experts(recv, rows_ref, wide_ref, down_ref, out):
    gather_rows(recv, rows_ref)
    width = recv[0].shape[3]
    half = wide_ref.shape[1] // 2
    both = jnp.dot(rows_ref[...], wide_ref[...], preferred_element_type=F32)
    gate, up = both[:, :half], both[:, half:]
    hidden = (gate / (1.0 + jnp.exp(-gate)) * up).astype(BF)
    tail = None
    for q in range(QUARTERS):
        value = jnp.dot(hidden, down_ref[:, quarter(q, width)], preferred_element_type=F32)
        tail = store_for_source(out[0], q, value, tail)
    out[1][...] = tail.reshape(out[1].shape).astype(BF)


def backward_experts(recv, recv_grad, rows_ref, grads_ref, wide_ref, down_ref, out):
    gather_rows(recv, rows_ref)
    gather_rows(recv_grad, grads_ref)
    width = recv[0].shape[3]
    half = wide_ref.shape[1] // 2
    last = (((1,), (1,)), ((), ()))
    both = jnp.dot(rows_ref[...], wide_ref[...], preferred_element_type=F32)
    gate, up = both[:, :half], both[:, half:]
    down = lax.dot_general(grads_ref[...], down_ref[...], last, preferred_element_type=F32)
    sigmoid = 1.0 / (1.0 + jnp.exp(-gate))
    grads = jnp.concatenate(
        [
            (down * up * (sigmoid * (1.0 + gate * (1.0 - sigmoid)))).astype(BF),
            (down * (gate * sigmoid)).astype(BF),
        ],
        axis=1,
    )
    tail = None
    for q in range(QUARTERS):
        value = lax.dot_general(
            grads, wide_ref[quarter(q, width)], last, preferred_element_type=F32
        )
        tail = store_for_source(out[0], q, value, tail)
    out[1][...] = tail.reshape(out[1].shape).astype(BF)


def front_last_kernel(
    middle_hbm, back_hbm, meta_hbm, done_hbm, out_hbm, done_out,
    middle_ref, back_ref, meta_ref, out_ref, done_ref, sem,
):
    width = back_ref.shape[3]
    experts = back_ref.shape[0] * 2
    pairs = (
        (meta_hbm, meta_ref), (back_hbm, back_ref), (middle_hbm, middle_ref), (done_hbm, done_ref),
    )
    copies = [pltpu.make_async_copy(a, b, sem.at[i]) for i, (a, b) in enumerate(pairs)]
    for copy in copies:
        copy.start()
    for copy in copies:
        copy.wait()
    copies = [pltpu.make_async_copy(done_ref, done_out, sem.at[4])]
    copies[0].start()
    gate = as_column(meta_ref[0:1])
    rows_of = unpack(meta_ref[1:2].astype(jnp.int32), experts, back_ref)
    for q in range(QUARTERS):
        cols = quarter(q, width)
        out_ref[:, cols] = (middle_ref[:, cols].astype(F32) + gate * rows_of(q)).astype(BF)
        copy = pltpu.make_async_copy(out_ref.at[:, cols], out_hbm.at[:, cols], sem.at[5 + q])
        copy.start()
        copies.append(copy)
    for copy in copies:
        copy.wait()


def back_last(mid_ref, grad_ref, gain_ref, back_ref, meta_ref, out_ref, amount):
    experts = back_ref.shape[0] * 2
    width = back_ref.shape[3]
    tokens, features = mid_ref.shape
    rows_of = unpack(meta_ref[1:2].astype(jnp.int32), experts, back_ref)
    squares = jnp.zeros((tokens, 1), F32)
    products = jnp.zeros((tokens, 1), F32)
    for q in range(QUARTERS):
        cols = quarter(q, width)
        mid = mid_ref[:, cols].astype(F32)
        value = gain_ref[:, cols] * rows_of(q)
        amount[:, cols] = value
        squares += jnp.sum(mid * mid, axis=-1, keepdims=True)
        products += jnp.sum(mid * value, axis=-1, keepdims=True)
    scale = lax.rsqrt(squares / features + EPS)
    factor = scale * scale * scale * (products / features)
    for q in range(QUARTERS):
        cols = quarter(q, width)
        out_ref[:, cols] = (
            grad_ref[:, cols].astype(F32)
            + scale * amount[:, cols]
            - mid_ref[:, cols].astype(F32) * factor
        ).astype(BF)


def place():
    section, index = lax.axis_index("section"), lax.axis_index("expert")
    return section, index // (2 * NX), (index // 2) % NX, index % 2


def device(section, z, x, core):
    return (section, (z * NX + x) * 2 + core)


def far_first(planes):
    return sorted(range(1, planes), key=lambda d: -min(d, planes - d))


def stages_of(planes):
    return [sorted({d, planes - d}) for d in range(1, planes // 2 + 1)]


class Flow:
    def __init__(self, items, depth):
        self.unsent = list(items)
        self.waiting = []
        self.depth = depth

    def fill(self):
        while self.unsent and self.sent < self.depth:
            one, d = self.unsent.pop(0)
            one.send(d)
            self.waiting.append((one, d))
            self.sent += 1

    def open(self):
        self.sent = 0
        self.fill()

    def more(self, items):
        self.unsent += items
        self.fill()

    def left(self):
        return len(self.waiting) + len(self.unsent)

    def turn(self, count=1):
        for _ in range(count):
            one, d = self.waiting.pop(0)
            self.sent -= 1
            self.fill()
            one.forward(d)


def greet(targets):
    barrier = pltpu.get_barrier_semaphore()
    for target in targets:
        pl.semaphore_signal(barrier, inc=1, device_id=target, device_id_type=MESH)
    pl.semaphore_wait(barrier, len(targets))


def remote(src, dst, send, recv, target):
    return pltpu.make_async_remote_copy(
        src_ref=src, dst_ref=dst, send_sem=send, recv_sem=recv,
        device_id=target, device_id_type=MESH,
    )


def dma(*shape):
    return pltpu.SemaphoreType.DMA(shape)


class Gather:
    def __init__(self, kv, zsend, zrecv, xsend, xrecv, csend, crecv):
        self.kv = kv
        self.sems = (zsend, zrecv, xsend, xrecv, csend, crecv)
        self.planes = kv[0].shape[1]
        self.started = []

    def go(self, ref, send, recv, target):
        copy = remote(ref, ref, send, recv, target)
        copy.start()
        self.started.append(copy)

    def along_x(self, h, origin, d):
        _, _, xsend, xrecv, _, _ = self.sems
        s, z, x, c = place()
        for dx in (2, 1, 3):
            self.go(
                self.kv[h].at[c, origin, x], xsend.at[h, d, dx - 1], xrecv.at[h, origin, x],
                device(s, z, (x + dx) % NX, c),
            )

    def await_x(self, h, origin, d):
        _, _, xsend, xrecv, _, _ = self.sems
        s, z, x, c = place()
        for dx in (1, 3, 2):
            ref = self.kv[h].at[c, origin, (x + dx) % NX]
            remote(
                ref, ref, xsend.at[h, d, dx - 1], xrecv.at[h, origin, (x + dx) % NX],
                device(s, z, (x + dx) % NX, c),
            ).wait_recv()

    def z_ref(self, h, origin):
        _, _, x, c = place()
        return self.kv[0].at[c, origin, x] if h == 0 else self.kv[1].at[c, origin]

    def along_z(self, h, d, way):
        zsend, zrecv = self.sems[:2]
        s, z, x, c = place()
        origin = (z - way * d + self.planes) % self.planes
        self.go(
            self.z_ref(h, origin), zsend.at[h, (way + 1) // 2, d], zrecv.at[h, origin],
            device(s, (z + way + self.planes) % self.planes, x, c),
        )

    def await_z(self, h, d, way):
        zsend, zrecv = self.sems[:2]
        s, z, x, c = place()
        origin = (z - way * d + self.planes) % self.planes
        ref = self.z_ref(h, origin)
        remote(
            ref, ref, zsend.at[h, (way + 1) // 2, d], zrecv.at[h, origin], device(s, origin, x, c)
        ).wait_recv()
        return origin

    def swap(self, h, origin):
        _, _, _, _, csend, crecv = self.sems
        s, z, x, c = place()
        self.go(
            self.kv[h].at[c, origin], csend.at[h, origin], crecv.at[h, origin],
            device(s, z, x, 1 - c),
        )

    def reach(self, way):
        return self.planes // 2 if way == 1 else (self.planes - 1) // 2

    def start(self):
        _, z, x, c = place()
        self.along_x(1, z, 0)
        for way in (1, -1):
            if self.reach(way) > 0:
                self.along_z(0, 0, way)
        self.along_x(0, z, 0)

    def turn(self):
        z = place()[1]
        self.await_x(1, z, 0)
        for way in (1, -1):
            if self.reach(way) > 0:
                self.along_z(1, 0, way)
        self.swap(1, z)

    def step(self, d):
        for h in (0, 1):
            for way in (1, -1):
                if d <= self.reach(way):
                    origin = self.await_z(h, d, way)
                    if d < self.reach(way):
                        self.along_z(h, d, way)
                    if h == 0:
                        self.along_x(0, origin, d if way == 1 else self.planes - d)
                    else:
                        self.swap(1, origin)

    def settle(self):
        z = place()[1]
        for d in range(self.planes // 2 + 1):
            for way in (1, -1):
                if d <= self.reach(way) and (d > 0 or way == 1):
                    origin = (z - way * d + self.planes) % self.planes
                    self.await_x(0, origin, d if way == 1 else self.planes - d)
                    self.swap(0, origin)

    def ready(self, h):
        _, _, _, _, csend, crecv = self.sems
        s, z, x, c = place()
        for k in range(self.planes):
            ref = self.kv[h].at[1 - c, k]
            remote(ref, ref, csend.at[h, k], crecv.at[h, k], device(s, z, x, 1 - c)).wait_recv()

    def drain(self):
        for copy in self.started:
            copy.wait_send()

    @staticmethod
    def scratch(planes):
        return [
            dma(2, 2, planes), dma(2, planes), dma(2, planes, NX - 1), dma(2, planes, NX),
            dma(2, planes), dma(2, planes),
        ]


def join(first, second, half):
    upper = iota(first.shape, 0) < 4
    if half == 0:
        return jnp.where(upper, first, pltpu.roll(second, 4, 0))
    return jnp.where(upper, pltpu.roll(first, 4, 0), second)


class Dispatch:
    def __init__(
        self, send_ref, zbuf, shared, main, tail, zsend, zrecv, xsend, xrecv, tsend, trecv, local
    ):
        self.refs = (send_ref, zbuf, shared, main, tail)
        self.sems = (zsend, zrecv, xsend, xrecv, tsend, trecv, local)
        self.planes = send_ref.shape[0]
        self.started = []
        self.local = []

    def send(self, d):
        send_ref, zbuf = self.refs[:2]
        zsend, zrecv = self.sems[:2]
        s, z, x, c = place()
        to = (z + d) % self.planes
        copy = remote(
            send_ref.at[to], zbuf.at[z], zsend.at[d], zrecv.at[z], device(s, to, x, c)
        )
        copy.start()
        self.started.append(copy)

    def send_stages(self, stages):
        for stage in stages:
            for d in stage:
                self.send(d)

    def forward_all(self, k):
        stages = stages_of(self.planes)
        for d in stages[k]:
            self.forward(d)
        for j in {0: (0,), 2: (1, 3), 3: (2,)}.get(k, ()):
            self.forward_tail(j)

    def forward(self, d):
        send_ref, zbuf, _, main, _ = self.refs
        zsend, zrecv, xsend, xrecv, _, _, local = self.sems
        s, z, x, c = place()
        origin = (z + d) % self.planes
        source = zbuf.at[origin]
        if d == 0:
            source = send_ref.at[z]
            zbuf[z, 4] = send_ref[z, 4]
        else:
            remote(
                send_ref.at[origin], zbuf.at[origin], zsend.at[d], zrecv.at[origin],
                device(s, origin, x, c),
            ).wait_recv()
        for dx in (2, 1, 3):
            to = (x + dx) % NX
            copy = remote(
                source.at[pl.ds(5 * (to // 2), 4)], main.at[x * self.planes + origin],
                xsend.at[dx - 1, d], xrecv.at[x, origin], device(s, z, to, c),
            )
            copy.start()
            self.started.append(copy)
        mine = pltpu.make_async_copy(
            source.at[pl.ds(5 * (x // 2), 4)], main.at[x * self.planes + origin], local.at[d]
        )
        mine.start()
        self.local.append(mine)

    def pair(self, j):
        half = self.planes // 2
        return (place()[1] // 2 + j) % half

    def forward_tail(self, j):
        _, zbuf, shared, _, tail = self.refs
        _, _, _, _, tsend, trecv, _ = self.sems
        s, z, x, c = place()
        half = self.planes // 2
        p = self.pair(j)
        first, second = zbuf[2 * p, 4].astype(F32), zbuf[2 * p + 1, 4].astype(F32)
        for h in range(2):
            shared[p, h] = join(first, second, h).astype(BF)
        for dx in (2, 1, 3):
            to = (x + dx) % NX
            copy = remote(
                shared.at[p, to // 2], tail.at[x * half + p], tsend.at[dx - 1, j],
                trecv.at[x, p], device(s, z, to, c),
            )
            copy.start()
            self.started.append(copy)
        tail[x * half + p] = shared[p, x // 2]

    def arrive(self):
        send_ref, zbuf, shared, main, tail = self.refs
        zsend, zrecv, xsend, xrecv, tsend, trecv, local = self.sems
        s, z, x, c = place()
        half = self.planes // 2
        for d in range(self.planes):
            origin = (z + d) % self.planes
            for dx in range(1, NX):
                source = (x + dx) % NX
                remote(
                    zbuf.at[origin, pl.ds(0, 4)], main.at[source * self.planes + origin],
                    xsend.at[dx - 1, d], xrecv.at[source, origin], device(s, z, source, c),
                ).wait_recv()
        for j in range(half):
            p = self.pair(j)
            for dx in range(1, NX):
                source = (x + dx) % NX
                remote(
                    shared.at[p, 0], tail.at[source * half + p], tsend.at[dx - 1, j],
                    trecv.at[source, p], device(s, z, source, c),
                ).wait_recv()
        for copy in self.local:
            copy.wait()

    def drain(self):
        for copy in self.started:
            copy.wait_send()

    @staticmethod
    def scratch(planes):
        half = planes // 2
        return [
            dma(planes), dma(planes), dma(NX - 1, planes), dma(NX, planes),
            dma(NX - 1, half), dma(NX, half), dma(planes),
        ]


class Return:
    def __init__(
        self, main, tail, pmain, ptail, stage, out_ref, by, xsend, xrecv, tsend, trecv, zsend, zrecv
    ):
        self.refs = (main, tail, pmain, ptail, stage, out_ref)
        self.sems = (xsend, xrecv, tsend, trecv, zsend, zrecv)
        self.planes = stage.shape[0]
        self.by = by
        self.started = []

    def order(self):
        half = self.planes // 2
        return sorted(range(half), key=lambda j: -min(j, half - j))

    def pair(self, j):
        half = self.planes // 2
        return (place()[1] // 2 + j) % half

    def messages(self, j, mine):
        main, tail, pmain, ptail, _, _ = self.refs
        xsend, xrecv, tsend, trecv, _, _ = self.sems
        half = self.planes // 2
        p = self.pair(j)
        for dx in (2, 1, 3):
            other = (place()[2] + dx) % NX
            left = other if mine else place()[2]
            spot = place()[2] if mine else other
            for k in range(2):
                origin = 2 * p + k
                yield (
                    main.at[left * self.planes + origin], pmain.at[spot * self.planes + origin],
                    xsend.at[dx - 1, 2 * j + k], xrecv.at[spot, origin], other,
                )
            yield (
                tail.at[left * half + p], ptail.at[spot * half + p],
                tsend.at[dx - 1, j], trecv.at[spot, p], other,
            )

    def send(self, j):
        s, z, x, c = place()
        for source, target, sent, came, other in self.messages(j, True):
            copy = remote(source, target, sent, came, device(s, z, other, c))
            copy.start()
            self.started.append(copy)

    def forward(self, j):
        main, tail, pmain, ptail, stage, out_ref = self.refs
        _, _, _, _, zsend, zrecv = self.sems
        s, z, x, c = place()
        half = self.planes // 2
        p = self.pair(j)
        for k in range(2):
            mine = x * self.planes + 2 * p + k
            pmain[mine] = main[mine]
        ptail[x * half + p] = tail[x * half + p]
        for source, target, sent, came, other in self.messages(j, False):
            remote(source, target, sent, came, device(s, z, other, c)).wait_recv()

        def last(source):
            return ptail[source * half + p].astype(F32)

        first, second = last(0) + last(1), last(2) + last(3)
        sections = lax.axis_size("section")
        for k in range(2):
            origin = 2 * p + k

            def piece(source, q):
                return pmain[source * self.planes + origin, q].astype(F32)

            for q in range(QUARTERS):
                stage[origin, q] = (piece(0, q) + piece(1, q)).astype(BF)
                stage[origin, 5 + q] = (piece(2, q) + piece(3, q)).astype(BF)
            stage[origin, 4] = join(first, second, k).astype(BF)
            copy = remote(
                stage.at[origin], out_ref.at[z], zsend.at[2 * j + k], zrecv.at[z],
                device((s + self.by + sections) % sections, origin, x, c),
            )
            copy.start()
            self.started.append(copy)

    def arrive(self):
        stage, out_ref = self.refs[4:]
        zsend, zrecv = self.sems[4:]
        s, z, x, c = place()
        sections = lax.axis_size("section")
        for d in range(self.planes):
            origin = (z + d) % self.planes
            remote(
                stage.at[origin], out_ref.at[origin], zsend.at[d], zrecv.at[origin],
                device((s - self.by + sections) % sections, origin, x, c),
            ).wait_recv()

    def drain(self):
        for copy in self.started:
            copy.wait_send()

    @staticmethod
    def scratch(planes):
        half = planes // 2
        return [
            dma(NX - 1, planes), dma(NX, planes), dma(NX - 1, half), dma(NX, half),
            dma(planes), dma(planes),
        ]


def everyone(planes, sections):
    s, z, x, c = place()
    peers = [device(s, (z + d) % planes, x, c) for d in range(1, planes)]
    peers += [device(s, z, (x + d) % NX, c) for d in range(1, NX)]
    peers += [
        device((s + by) % sections, (z + d) % planes, x, c)
        for by in (1, sections - 1) for d in range(planes)
    ]
    return peers + [device(s, z, x, 1 - c)]


def hand_over(refs, outs, send, recv, target):
    copies = []
    for i, (ref, out) in enumerate(zip(refs, outs)):
        copy = remote(ref, out, send.at[i], recv.at[i], target)
        copy.start()
        copies.append(copy)
    return copies


NAMES = (
    "mid", "grad", "query", "entry", "wide", "down", "expert0", "expert1",
    "kv0", "kv1", "total", "middle", "rows0", "rows1", "rows2", "zbuf0", "zbuf1", "zbuf2", "recv0",
    "recv1", "recv2", "part0", "part1", "pbuf0", "pbuf1", "stage0", "stage1", "back_in",
    "last0", "last1", "last2", "plast0", "plast1", "blast0", "blast1",
    "shared0", "shared1", "shared2",
    "mid_in", "grad_in", "gain_in", "b_meta", "f_meta", "b_meta_in", "result",
)


def main_kernel(
    sel, kv_in, gain, f_route, f_gate, b_route, b_gate,
    mid_hbm, grad_hbm, query_hbm, entry_hbm, wg, wu, wd,
    result_out, middle_out, f_meta_out, front_out,
    *scratch,
):
    v = dict(zip(NAMES, scratch))
    sems = list(scratch[len(NAMES) :])
    s, z, x, c = place()
    sections = lax.axis_size("section")
    planes = v["rows0"].shape[0]
    width = v["rows0"].shape[3]
    experts = planes * 2
    load, csend, crecv, ysend, yrecv = sems[:5]
    sems = sems[5:]
    kv = (v["kv0"], v["kv1"])
    gather = Gather(kv, *sems[:6])
    sends = [
        Dispatch(
            v[f"rows{i}"], v[f"zbuf{i}"], v[f"shared{i}"], v[f"recv{i}"], v[f"last{i}"],
            *sems[6 + 7 * i : 13 + 7 * i],
        )
        for i in range(3)
    ]
    ones, twos, front = sends
    back_ret, front_ret = [
        Return(
            v[f"part{i}"], v[f"plast{i}"], v[f"pbuf{i}"], v[f"blast{i}"], v[f"stage{i}"],
            (v["back_in"], front_out)[i], (-1, 1)[i], *sems[27 + 6 * i : 33 + 6 * i],
        )
        for i in range(2)
    ]

    local = []
    hidden = wg.shape[1]
    places = [v["wide"].at[:, pl.ds(k * hidden, hidden)] for k in range(4)]
    places += [v["down"].at[pl.ds(k * hidden, hidden)] for k in range(2)]
    targets = [v[name] for name in ("mid", "grad", "query", "entry")] + places[::2]
    for i, (source, target) in enumerate(
        zip((mid_hbm, grad_hbm, query_hbm, entry_hbm, wg, wu, wd), targets)
    ):
        copy = pltpu.make_async_copy(source, target, load.at[i])
        copy.start()
        local.append(copy)
    for head in range(KV_HEADS):
        for w in range(2):
            kv[head][c, z, x, w] = kv_in[w * KV_HEADS + head]
    for name, gate_ref, route_ref in (("b_meta", b_gate, b_route), ("f_meta", f_gate, f_route)):
        v[name][...] = jnp.zeros_like(v[name])
        v[name][0:1] = gate_ref[...]
        v[name][1:2] = route_ref[...].astype(F32)
    v["total"][...] = jnp.zeros_like(v["total"])
    greet(everyone(planes, sections))
    stages = stages_of(planes)
    gather.start()
    gather.turn()
    local[0].wait()
    pack(b_route[...], experts, normed_rows(v["mid"], gain, width), v["rows0"])
    ones.send_stages(stages[:1])
    ones.forward(0)
    gate = as_column(b_gate[...])
    local[1].wait()

    def scaled(q):
        return (gate * v["grad"][:, quarter(q, width)].astype(F32)).astype(BF)

    pack(b_route[...], experts, scaled, v["rows1"])
    before = device((s + sections - 1) % sections, z, x, c)
    after = device((s + 1) % sections, z, x, c)
    gather.step(1)
    ones.send_stages(stages[1:2])
    ones.forward_all(0)
    gather.step(2)
    ones.send_stages(stages[2:3])
    twos.forward(0)
    ones.forward_all(1)
    gather.step(3)
    ones.send_stages(stages[3:4])
    gather.step(4)
    twos.send_stages(stages)
    ones.forward_all(2)
    gather.settle()
    shipped = hand_over(
        (v["mid"], v["grad"], gain, v["b_meta"]),
        (v["mid_in"], v["grad_in"], v["gain_in"], v["b_meta_in"]),
        ysend.at[0], yrecv.at[0], before,
    )
    weights = hand_over(
        (wg, wu, wd), places[1::2], csend, crecv,
        device(s, z, x, 1 - c),
    )
    ones.forward_all(3)
    twos.forward_all(0)
    twos.forward_all(1)
    for copy in local[2:4]:
        copy.wait()
    blocks = v["query"].shape[0] // BLK
    first = lax.axis_index("expert") * blocks
    for head in (1, 0):
        gather.ready(head)
        for b in range(blocks):
            attend(b * KV_HEADS + head, first, sel, v["query"], kv, v["total"])
        if head == 1:
            twos.forward_all(2)
    for q in range(QUARTERS):
        cols = quarter(q, width)
        v["middle"][:, cols] = (
            v["entry"][:, cols].astype(F32) + v["total"][:, cols]
        ).astype(BF)
    pack(f_route[...], experts, normed_rows(v["middle"], gain, width), v["rows2"])
    front.send_stages(stages)
    front.forward(0)
    twos.forward_all(3)
    shipped += hand_over(
        (v["middle"], v["f_meta"]), (middle_out, f_meta_out), ysend.at[1], yrecv.at[1], after
    )
    front.forward_all(0)
    ones.arrive()
    twos.arrive()
    for copy in local[4:]:
        copy.wait()
    for copy in weights:
        copy.wait()
    backward_experts(
        (v["recv0"], v["last0"]), (v["recv1"], v["last1"]), v["expert0"], v["expert1"],
        v["wide"], v["down"], (v["part0"], v["plast0"]),
    )
    turns = back_ret.order()
    flow = Flow([(back_ret, d) for d in turns], 2)
    flow.open()
    front.forward_all(1)
    front.forward_all(2)
    flow.turn()
    front.forward_all(3)
    flow.turn()
    front.arrive()
    forward_experts(
        (v["recv2"], v["last2"]), v["expert0"], v["wide"], v["down"], (v["part1"], v["plast1"])
    )
    flow.more([(front_ret, d) for d in turns])
    flow.turn(flow.left() - len(turns) // 2)
    back_ret.arrive()
    for copy in shipped:
        copy.wait()
    back_last(
        v["mid_in"], v["grad_in"], v["gain_in"], v["back_in"], v["b_meta_in"],
        v["result"], v["total"],
    )
    last = pltpu.make_async_copy(v["result"], result_out, load.at[7])
    last.start()
    flow.turn(flow.left())
    front_ret.arrive()
    last.wait()
    for one in (gather, ones, twos, front, back_ret, front_ret):
        one.drain()


ANY = pl.BlockSpec(memory_space=pl.ANY)
VMEM = pl.BlockSpec(memory_space=pltpu.VMEM)
SMEM = pl.BlockSpec(memory_space=pltpu.SMEM)


def shards(
    front_input, queries, keys_values, selected_blocks, front_route, front_gate,
    back_middle, back_grad, back_route, back_gate, norm_gain, gate_slice, up_slice, down_slice,
):
    tokens, features = front_input.shape[1:]
    planes = lax.axis_size("expert") // (2 * NX)
    width = features // QUARTERS
    kv = keys_values[0].T.reshape(2 * KV_HEADS, HEAD_DIM, tokens)
    message = pltpu.VMEM((planes, 9, 8, width), BF)
    arrived = pltpu.VMEM((NX * planes, QUARTERS, 8, width), BF)
    lasts = pltpu.VMEM((NX * planes // 2, 8, width), BF)
    rows = pltpu.VMEM((tokens, features), BF)
    many = pltpu.VMEM((NX * planes * 9, features), BF)
    meta = pltpu.VMEM((8, tokens), F32)
    half_kv = pltpu.VMEM((2, planes, NX, 2, HEAD_DIM, tokens), BF)
    shapes = dict(
        mid=rows, grad=rows, query=rows, entry=rows,
        wide=pltpu.VMEM((features, 4 * gate_slice.shape[3]), BF),
        down=pltpu.VMEM((2 * gate_slice.shape[3], features), BF),
        expert0=many, expert1=many, kv0=half_kv, kv1=half_kv,
        total=pltpu.VMEM((tokens, features), F32), middle=rows,
        back_in=message, mid_in=rows, grad_in=rows, gain_in=pltpu.VMEM((1, features), F32),
        b_meta=meta, f_meta=meta, b_meta_in=meta, result=rows,
    )
    for i in range(3):
        shapes[f"rows{i}"] = shapes[f"zbuf{i}"] = message
        shapes[f"recv{i}"] = shapes[f"part{i}"] = shapes[f"pbuf{i}"] = arrived
        shapes[f"stage{i}"] = message
        shapes[f"last{i}"] = shapes[f"plast{i}"] = shapes[f"blast{i}"] = lasts
        shapes[f"shared{i}"] = pltpu.VMEM((planes // 2, 2, 8, width), BF)
    result, middle, f_meta, front = pl.pallas_call(
        main_kernel,
        out_shape=[
            jax.ShapeDtypeStruct((tokens, features), BF),
            jax.ShapeDtypeStruct((tokens, features), BF),
            jax.ShapeDtypeStruct((8, tokens), F32),
            jax.ShapeDtypeStruct((planes, 9, 8, width), BF),
        ],
        in_specs=[SMEM] + [VMEM] * 6 + [ANY] * 7,
        out_specs=[ANY] * 4,
        scratch_shapes=[shapes[name] for name in NAMES]
        + [dma(8), dma(3), dma(3), dma(2, 4), dma(2, 4)]
        + Gather.scratch(planes) + Dispatch.scratch(planes) * 3 + Return.scratch(planes) * 2,
        compiler_params=pltpu.CompilerParams(
            collective_id=0, has_side_effects=True, vmem_limit_bytes=63 << 20
        ),
        name="layer",
    )(
        selected_blocks[0], kv, norm_gain,
        front_route.reshape(1, tokens), front_gate.reshape(1, tokens),
        back_route.reshape(1, tokens), back_gate.reshape(1, tokens),
        back_middle[0], back_grad[0], queries[0], front_input[0],
        gate_slice[0, 0], up_slice[0, 0], down_slice[0, 0],
    )
    front_output, back_output = pl.pallas_call(
        front_last_kernel,
        out_shape=[jax.ShapeDtypeStruct((tokens, features), BF)] * 2,
        in_specs=[ANY] * 4,
        out_specs=[ANY] * 2,
        scratch_shapes=[rows, message, meta, rows, rows, dma(5 + QUARTERS)],
        compiler_params=pltpu.CompilerParams(vmem_limit_bytes=63 << 20),
        name="front_last",
    )(middle, front, f_meta, result)
    return (front_output[None], back_output[None])


def solution(mesh):
    rows = P("section", "expert", None)
    wide = P("section", "expert", None, None)
    return jax.shard_map(
        shards,
        mesh=mesh,
        in_specs=(rows, rows, rows, wide, rows, rows, rows, rows, rows, rows,
                  P("section", None), wide, wide, wide),
        out_specs=(rows, rows),
        check_vma=False,
    )
```

```python
import jax
import jax.numpy as jnp
from jax import lax
from jax.experimental import pallas as pl
from jax.experimental.pallas import tpu as pltpu
from jax.sharding import PartitionSpec as P

HEADS = 32
HEAD_DIM = 112
KV_HEADS = 2
GROUPS = HEADS // KV_HEADS
BLK = 64
SEL = 4
QUARTERS = 4
NX = 4
EPS = 1e-06
NEG = -1e30
MESH = pl.DeviceIdType.MESH
BF = jnp.bfloat16
F32 = jnp.float32


def iota(shape, dim):
    return lax.broadcasted_iota(jnp.int32, shape, dim)


def slot_row(route, experts):
    tokens = route.shape[1]
    onehot = jnp.where(iota((experts, tokens), 0) == route, 1.0, 0.0)
    earlier = jnp.where(iota((tokens, tokens), 0) < iota((tokens, tokens), 1), 1.0, 0.0)
    before = jnp.dot(onehot.astype(BF), earlier.astype(BF), preferred_element_type=F32)
    return jnp.sum(before * onehot, axis=0, keepdims=True).astype(jnp.int32)


def main_onehot(route, slot, experts):
    place = jnp.where(slot < 8, route * 8 + slot, -1)
    return jnp.where(iota((experts * 8, route.shape[1]), 0) == place, 1.0, 0.0)


def tail_onehot(route, slot, experts, quarter):
    place = jnp.where(slot >= 8, route * 4 + quarter, -1)
    return jnp.where(iota((experts * 4, route.shape[1]), 0) == place, 1.0, 0.0)


def pack(route, experts, rows_of, send_ref):
    slot = slot_row(route, experts)
    main = main_onehot(route, slot, experts).astype(BF)
    planes = experts // 2
    tail = None
    for q in range(QUARTERS):
        rows = rows_of(q)
        width = rows.shape[1]
        sorted_rows = jnp.dot(main, rows, preferred_element_type=F32).reshape(planes, 2, 8, width)
        send_ref[:, q] = sorted_rows[:, 0].astype(BF)
        send_ref[:, 5 + q] = sorted_rows[:, 1].astype(BF)
        last = jnp.dot(
            tail_onehot(route, slot, experts, q).astype(BF), rows, preferred_element_type=F32
        )
        tail = last if tail is None else tail + last
    send_ref[:, 4] = tail.reshape(planes, 8, width).astype(BF)


def unpack(route, experts, back_ref):
    slot = slot_row(route, experts)
    main = main_onehot(route, slot, experts).T.astype(BF)
    planes = experts // 2
    width = back_ref.shape[3]

    def rows_of(q):
        first = back_ref[:, q].astype(F32)
        second = back_ref[:, 5 + q].astype(F32)
        both = jnp.stack([first, second], axis=1).reshape(experts * 8, width).astype(BF)
        last = back_ref[:, 4].astype(F32).reshape(planes * 8, width).astype(BF)
        tail = tail_onehot(route, slot, experts, q).T.astype(BF)
        return jnp.dot(main, both, preferred_element_type=F32) + jnp.dot(
            tail, last, preferred_element_type=F32
        )

    return rows_of


def quarter(q, width):
    return slice(q * width, (q + 1) * width)


def normed_rows(ref, gain_ref, width):
    tokens, features = ref.shape
    squares = jnp.zeros((tokens, 1), F32)
    for q in range(QUARTERS):
        part = ref[:, quarter(q, width)].astype(F32)
        squares += jnp.sum(part * part, axis=-1, keepdims=True)
    scale = lax.rsqrt(squares / features + EPS)

    def rows_of(q):
        cols = quarter(q, width)
        return (ref[:, cols].astype(F32) * scale * gain_ref[:, cols]).astype(BF)

    return rows_of


def as_column(row):
    count = row.shape[1]
    return jnp.broadcast_to(row, (count, count)).T[:, 0:1]


def attend(pair, first, sel_ref, query_ref, kv_ref, total):
    b, h = pair // KV_HEADS, pair % KV_HEADS
    keys = SEL * BLK
    blocks = query_ref.shape[0] // BLK
    token_rows = slice(b * BLK, (b + 1) * BLK)
    chosen = [sel_ref[b, h, k] for k in range(SEL)]
    held = [[], []]
    for k in range(SEL):
        owner = chosen[k] // blocks
        spot = (owner % 2, owner // (2 * NX), (owner // 2) % NX)
        for w in range(2):
            held[w].append(kv_ref[h][(*spot, w)])
    lane = iota((2 * BLK, keys), 1)
    key_pos = lane % BLK
    at, to = iota((blocks * BLK, keys), 0), iota((blocks * BLK, keys), 1)
    picks = []
    for k in range(SEL):
        key_pos = key_pos + jnp.where(lane // BLK == k, chosen[k] * BLK, 0)
        inside = (at == to % BLK + (chosen[k] % blocks) * BLK) & (to // BLK == k)
        picks.append(jnp.where(inside, 1.0, 0.0).astype(BF))
    allowed = key_pos <= (first + b) * BLK + iota((2 * BLK, keys), 0) % BLK

    def selected(pieces):
        out = None
        for piece, pick in zip(pieces, picks):
            more = jnp.dot(piece, pick, preferred_element_type=F32)
            out = more if out is None else out + more
        return out.astype(BF)

    key_cols, value_cols = selected(held[0]), selected(held[1])
    for g in range(GROUPS // 2):
        offset = (HEAD_DIM * g) % 128
        window = 128 if offset + HEAD_DIM <= 128 else 256
        shift = jnp.where(
            iota((window, HEAD_DIM), 0) == iota((window, HEAD_DIM), 1) + offset, 1.0, 0.0
        ).astype(BF)
        key_moved = jnp.dot(shift, key_cols, preferred_element_type=F32).astype(BF)
        value_moved = jnp.dot(shift, value_cols, preferred_element_type=F32).astype(BF)
        starts = [
            HEAD_DIM * (h * GROUPS + g + half * (GROUPS // 2)) // 128 * 128 for half in range(2)
        ]
        query = jnp.concatenate([query_ref[token_rows, s : s + window] for s in starts], axis=0)
        scores = jnp.dot(query, key_moved, preferred_element_type=F32) * HEAD_DIM ** (-0.5)
        scores = jnp.where(allowed, scores, NEG)
        exp_scores = jnp.exp(scores - jnp.max(scores, axis=-1, keepdims=True))
        weights = exp_scores * (1.0 / jnp.sum(exp_scores, axis=-1, keepdims=True))
        mixed = lax.dot_general(
            weights.astype(BF), value_moved, (((1,), (1,)), ((), ())), preferred_element_type=F32
        )
        for half, s in enumerate(starts):
            total[token_rows, s : s + window] += mixed[half * BLK : (half + 1) * BLK]

def tail_select(count, q):
    row, col = iota((count, count * 4), 0), iota((count, count * 4), 1)
    return jnp.where(col == row * 4 + q, 1.0, 0.0).astype(BF)


def gather_rows(recv, rows_ref):
    main_ref, tail_ref = recv
    count, width = main_ref.shape[0], main_ref.shape[3]
    last = tail_ref[...].astype(F32).reshape(count * 4, width).astype(BF)
    for q in range(QUARTERS):
        cols = quarter(q, width)
        rows_ref[: count * 8, cols] = (
            main_ref[:, q].astype(F32).reshape(count * 8, width).astype(BF)
        )
        rows_ref[count * 8 :, cols] = jnp.dot(
            tail_select(count, q), last, preferred_element_type=F32
        ).astype(BF)


def store_for_source(main_ref, q, value, tail_total):
    count, width = main_ref.shape[0], main_ref.shape[3]
    main_ref[:, q] = value[: count * 8].reshape(count, 8, width).astype(BF)
    spread = lax.dot_general(
        tail_select(count, q), value[count * 8 :].astype(BF),
        (((0,), (0,)), ((), ())), preferred_element_type=F32,
    )
    return spread if tail_total is None else tail_total + spread


def forward_experts(recv, rows_ref, wide_ref, down_ref, out):
    gather_rows(recv, rows_ref)
    width = recv[0].shape[3]
    half = wide_ref.shape[1] // 2
    both = jnp.dot(rows_ref[...], wide_ref[...], preferred_element_type=F32)
    gate, up = both[:, :half], both[:, half:]
    hidden = (gate / (1.0 + jnp.exp(-gate)) * up).astype(BF)
    tail = None
    for q in range(QUARTERS):
        value = jnp.dot(hidden, down_ref[:, quarter(q, width)], preferred_element_type=F32)
        tail = store_for_source(out[0], q, value, tail)
    out[1][...] = tail.reshape(out[1].shape).astype(BF)


def backward_experts(recv, recv_grad, rows_ref, grads_ref, wide_ref, down_ref, out):
    gather_rows(recv, rows_ref)
    gather_rows(recv_grad, grads_ref)
    width = recv[0].shape[3]
    half = wide_ref.shape[1] // 2
    last = (((1,), (1,)), ((), ()))
    both = jnp.dot(rows_ref[...], wide_ref[...], preferred_element_type=F32)
    gate, up = both[:, :half], both[:, half:]
    down = lax.dot_general(grads_ref[...], down_ref[...], last, preferred_element_type=F32)
    sigmoid = 1.0 / (1.0 + jnp.exp(-gate))
    grads = jnp.concatenate(
        [
            (down * up * (sigmoid * (1.0 + gate * (1.0 - sigmoid)))).astype(BF),
            (down * (gate * sigmoid)).astype(BF),
        ],
        axis=1,
    )
    tail = None
    for q in range(QUARTERS):
        value = lax.dot_general(
            grads, wide_ref[quarter(q, width)], last, preferred_element_type=F32
        )
        tail = store_for_source(out[0], q, value, tail)
    out[1][...] = tail.reshape(out[1].shape).astype(BF)


def front_last_kernel(
    middle_hbm, back_hbm, meta_hbm, done_hbm, out_hbm, done_out,
    middle_ref, back_ref, meta_ref, out_ref, done_ref, sem,
):
    width = back_ref.shape[3]
    experts = back_ref.shape[0] * 2
    pairs = (
        (meta_hbm, meta_ref), (back_hbm, back_ref), (middle_hbm, middle_ref), (done_hbm, done_ref),
    )
    copies = [pltpu.make_async_copy(a, b, sem.at[i]) for i, (a, b) in enumerate(pairs)]
    for copy in copies:
        copy.start()
    for copy in copies:
        copy.wait()
    copies = [pltpu.make_async_copy(done_ref, done_out, sem.at[4])]
    copies[0].start()
    gate = as_column(meta_ref[0:1])
    rows_of = unpack(meta_ref[1:2].astype(jnp.int32), experts, back_ref)
    for q in range(QUARTERS):
        cols = quarter(q, width)
        out_ref[:, cols] = (middle_ref[:, cols].astype(F32) + gate * rows_of(q)).astype(BF)
        copy = pltpu.make_async_copy(out_ref.at[:, cols], out_hbm.at[:, cols], sem.at[5 + q])
        copy.start()
        copies.append(copy)
    for copy in copies:
        copy.wait()


def back_last(mid_ref, grad_ref, gain_ref, back_ref, meta_ref, out_ref, amount):
    experts = back_ref.shape[0] * 2
    width = back_ref.shape[3]
    tokens, features = mid_ref.shape
    rows_of = unpack(meta_ref[1:2].astype(jnp.int32), experts, back_ref)
    squares = jnp.zeros((tokens, 1), F32)
    products = jnp.zeros((tokens, 1), F32)
    for q in range(QUARTERS):
        cols = quarter(q, width)
        mid = mid_ref[:, cols].astype(F32)
        value = gain_ref[:, cols] * rows_of(q)
        amount[:, cols] = value
        squares += jnp.sum(mid * mid, axis=-1, keepdims=True)
        products += jnp.sum(mid * value, axis=-1, keepdims=True)
    scale = lax.rsqrt(squares / features + EPS)
    factor = scale * scale * scale * (products / features)
    for q in range(QUARTERS):
        cols = quarter(q, width)
        out_ref[:, cols] = (
            grad_ref[:, cols].astype(F32)
            + scale * amount[:, cols]
            - mid_ref[:, cols].astype(F32) * factor
        ).astype(BF)


def place():
    section, index = lax.axis_index("section"), lax.axis_index("expert")
    return section, index // (2 * NX), (index // 2) % NX, index % 2


def device(section, z, x, core):
    return (section, (z * NX + x) * 2 + core)


def far_first(planes):
    return sorted(range(1, planes), key=lambda d: -min(d, planes - d))


def stages_of(planes):
    return [sorted({d, planes - d}) for d in range(1, planes // 2 + 1)]


class Flow:
    def __init__(self, items, depth):
        self.unsent = list(items)
        self.waiting = []
        self.depth = depth

    def fill(self):
        while self.unsent and self.sent < self.depth:
            one, d = self.unsent.pop(0)
            one.send(d)
            self.waiting.append((one, d))
            self.sent += 1

    def open(self):
        self.sent = 0
        self.fill()

    def more(self, items):
        self.unsent += items
        self.fill()

    def left(self):
        return len(self.waiting) + len(self.unsent)

    def turn(self, count=1):
        for _ in range(count):
            one, d = self.waiting.pop(0)
            self.sent -= 1
            self.fill()
            one.forward(d)


def greet(targets):
    barrier = pltpu.get_barrier_semaphore()
    for target in targets:
        pl.semaphore_signal(barrier, inc=1, device_id=target, device_id_type=MESH)
    pl.semaphore_wait(barrier, len(targets))


def remote(src, dst, send, recv, target):
    return pltpu.make_async_remote_copy(
        src_ref=src, dst_ref=dst, send_sem=send, recv_sem=recv,
        device_id=target, device_id_type=MESH,
    )


def dma(*shape):
    return pltpu.SemaphoreType.DMA(shape)


class Gather:
    def __init__(self, kv, zsend, zrecv, xsend, xrecv, csend, crecv):
        self.kv = kv
        self.sems = (zsend, zrecv, xsend, xrecv, csend, crecv)
        self.planes = kv[0].shape[1]
        self.started = []

    def go(self, ref, send, recv, target):
        copy = remote(ref, ref, send, recv, target)
        copy.start()
        self.started.append(copy)

    def along_x(self, h, origin, d):
        _, _, xsend, xrecv, _, _ = self.sems
        s, z, x, c = place()
        for dx in (2, 1, 3):
            self.go(
                self.kv[h].at[c, origin, x], xsend.at[h, d, dx - 1], xrecv.at[h, origin, x],
                device(s, z, (x + dx) % NX, c),
            )

    def await_x(self, h, origin, d):
        _, _, xsend, xrecv, _, _ = self.sems
        s, z, x, c = place()
        for dx in (1, 3, 2):
            ref = self.kv[h].at[c, origin, (x + dx) % NX]
            remote(
                ref, ref, xsend.at[h, d, dx - 1], xrecv.at[h, origin, (x + dx) % NX],
                device(s, z, (x + dx) % NX, c),
            ).wait_recv()

    def z_ref(self, h, origin):
        _, _, x, c = place()
        return self.kv[0].at[c, origin, x] if h == 0 else self.kv[1].at[c, origin]

    def along_z(self, h, d, way):
        zsend, zrecv = self.sems[:2]
        s, z, x, c = place()
        origin = (z - way * d + self.planes) % self.planes
        self.go(
            self.z_ref(h, origin), zsend.at[h, (way + 1) // 2, d], zrecv.at[h, origin],
            device(s, (z + way + self.planes) % self.planes, x, c),
        )

    def await_z(self, h, d, way):
        zsend, zrecv = self.sems[:2]
        s, z, x, c = place()
        origin = (z - way * d + self.planes) % self.planes
        ref = self.z_ref(h, origin)
        remote(
            ref, ref, zsend.at[h, (way + 1) // 2, d], zrecv.at[h, origin], device(s, origin, x, c)
        ).wait_recv()
        return origin

    def swap(self, h, origin):
        _, _, _, _, csend, crecv = self.sems
        s, z, x, c = place()
        self.go(
            self.kv[h].at[c, origin], csend.at[h, origin], crecv.at[h, origin],
            device(s, z, x, 1 - c),
        )

    def reach(self, way):
        return self.planes // 2 if way == 1 else (self.planes - 1) // 2

    def start(self):
        _, z, x, c = place()
        self.along_x(1, z, 0)
        for way in (1, -1):
            if self.reach(way) > 0:
                self.along_z(0, 0, way)
        self.along_x(0, z, 0)

    def turn(self):
        z = place()[1]
        self.await_x(1, z, 0)
        for way in (1, -1):
            if self.reach(way) > 0:
                self.along_z(1, 0, way)
        self.swap(1, z)

    def step(self, d):
        for h in (0, 1):
            for way in (1, -1):
                if d <= self.reach(way):
                    origin = self.await_z(h, d, way)
                    if d < self.reach(way):
                        self.along_z(h, d, way)
                    if h == 0:
                        self.along_x(0, origin, d if way == 1 else self.planes - d)
                    else:
                        self.swap(1, origin)

    def settle(self):
        z = place()[1]
        for d in range(self.planes // 2 + 1):
            for way in (1, -1):
                if d <= self.reach(way) and (d > 0 or way == 1):
                    origin = (z - way * d + self.planes) % self.planes
                    self.await_x(0, origin, d if way == 1 else self.planes - d)
                    self.swap(0, origin)

    def ready(self, h):
        _, _, _, _, csend, crecv = self.sems
        s, z, x, c = place()
        for k in range(self.planes):
            ref = self.kv[h].at[1 - c, k]
            remote(ref, ref, csend.at[h, k], crecv.at[h, k], device(s, z, x, 1 - c)).wait_recv()

    def drain(self):
        for copy in self.started:
            copy.wait_send()

    @staticmethod
    def scratch(planes):
        return [
            dma(2, 2, planes), dma(2, planes), dma(2, planes, NX - 1), dma(2, planes, NX),
            dma(2, planes), dma(2, planes),
        ]


def join(first, second, half):
    upper = iota(first.shape, 0) < 4
    if half == 0:
        return jnp.where(upper, first, pltpu.roll(second, 4, 0))
    return jnp.where(upper, pltpu.roll(first, 4, 0), second)


class Dispatch:
    def __init__(
        self, send_ref, zbuf, shared, main, tail, zsend, zrecv, xsend, xrecv, tsend, trecv, local
    ):
        self.refs = (send_ref, zbuf, shared, main, tail)
        self.sems = (zsend, zrecv, xsend, xrecv, tsend, trecv, local)
        self.planes = send_ref.shape[0]
        self.started = []
        self.local = []

    def send(self, d):
        send_ref, zbuf = self.refs[:2]
        zsend, zrecv = self.sems[:2]
        s, z, x, c = place()
        to = (z + d) % self.planes
        copy = remote(
            send_ref.at[to], zbuf.at[z], zsend.at[d], zrecv.at[z], device(s, to, x, c)
        )
        copy.start()
        self.started.append(copy)

    def send_stages(self, stages):
        for stage in stages:
            for d in stage:
                self.send(d)

    def forward_all(self, k):
        stages = stages_of(self.planes)
        for d in stages[k]:
            self.forward(d)
        for j in {0: (0,), 2: (1, 3), 3: (2,)}.get(k, ()):
            self.forward_tail(j)

    def forward(self, d):
        send_ref, zbuf, _, main, _ = self.refs
        zsend, zrecv, xsend, xrecv, _, _, local = self.sems
        s, z, x, c = place()
        origin = (z + d) % self.planes
        source = zbuf.at[origin]
        if d == 0:
            source = send_ref.at[z]
            zbuf[z, 4] = send_ref[z, 4]
        else:
            remote(
                send_ref.at[origin], zbuf.at[origin], zsend.at[d], zrecv.at[origin],
                device(s, origin, x, c),
            ).wait_recv()
        for dx in (2, 1, 3):
            to = (x + dx) % NX
            copy = remote(
                source.at[pl.ds(5 * (to // 2), 4)], main.at[x * self.planes + origin],
                xsend.at[dx - 1, d], xrecv.at[x, origin], device(s, z, to, c),
            )
            copy.start()
            self.started.append(copy)
        mine = pltpu.make_async_copy(
            source.at[pl.ds(5 * (x // 2), 4)], main.at[x * self.planes + origin], local.at[d]
        )
        mine.start()
        self.local.append(mine)

    def pair(self, j):
        half = self.planes // 2
        return (place()[1] // 2 + j) % half

    def forward_tail(self, j):
        _, zbuf, shared, _, tail = self.refs
        _, _, _, _, tsend, trecv, _ = self.sems
        s, z, x, c = place()
        half = self.planes // 2
        p = self.pair(j)
        first, second = zbuf[2 * p, 4].astype(F32), zbuf[2 * p + 1, 4].astype(F32)
        for h in range(2):
            shared[p, h] = join(first, second, h).astype(BF)
        for dx in (2, 1, 3):
            to = (x + dx) % NX
            copy = remote(
                shared.at[p, to // 2], tail.at[x * half + p], tsend.at[dx - 1, j],
                trecv.at[x, p], device(s, z, to, c),
            )
            copy.start()
            self.started.append(copy)
        tail[x * half + p] = shared[p, x // 2]

    def arrive(self):
        send_ref, zbuf, shared, main, tail = self.refs
        zsend, zrecv, xsend, xrecv, tsend, trecv, local = self.sems
        s, z, x, c = place()
        half = self.planes // 2
        for d in range(self.planes):
            origin = (z + d) % self.planes
            for dx in range(1, NX):
                source = (x + dx) % NX
                remote(
                    zbuf.at[origin, pl.ds(0, 4)], main.at[source * self.planes + origin],
                    xsend.at[dx - 1, d], xrecv.at[source, origin], device(s, z, source, c),
                ).wait_recv()
        for j in range(half):
            p = self.pair(j)
            for dx in range(1, NX):
                source = (x + dx) % NX
                remote(
                    shared.at[p, 0], tail.at[source * half + p], tsend.at[dx - 1, j],
                    trecv.at[source, p], device(s, z, source, c),
                ).wait_recv()
        for copy in self.local:
            copy.wait()

    def drain(self):
        for copy in self.started:
            copy.wait_send()

    @staticmethod
    def scratch(planes):
        half = planes // 2
        return [
            dma(planes), dma(planes), dma(NX - 1, planes), dma(NX, planes),
            dma(NX - 1, half), dma(NX, half), dma(planes),
        ]


class Return:
    def __init__(
        self, main, tail, pmain, ptail, stage, out_ref, by, xsend, xrecv, tsend, trecv, zsend, zrecv
    ):
        self.refs = (main, tail, pmain, ptail, stage, out_ref)
        self.sems = (xsend, xrecv, tsend, trecv, zsend, zrecv)
        self.planes = stage.shape[0]
        self.by = by
        self.started = []

    def order(self):
        half = self.planes // 2
        return sorted(range(half), key=lambda j: -min(j, half - j))

    def pair(self, j):
        half = self.planes // 2
        return (place()[1] // 2 + j) % half

    def messages(self, j, mine):
        main, tail, pmain, ptail, _, _ = self.refs
        xsend, xrecv, tsend, trecv, _, _ = self.sems
        half = self.planes // 2
        p = self.pair(j)
        for dx in (2, 1, 3):
            other = (place()[2] + dx) % NX
            left = other if mine else place()[2]
            spot = place()[2] if mine else other
            for k in range(2):
                origin = 2 * p + k
                yield (
                    main.at[left * self.planes + origin], pmain.at[spot * self.planes + origin],
                    xsend.at[dx - 1, 2 * j + k], xrecv.at[spot, origin], other,
                )
            yield (
                tail.at[left * half + p], ptail.at[spot * half + p],
                tsend.at[dx - 1, j], trecv.at[spot, p], other,
            )

    def send(self, j):
        s, z, x, c = place()
        for source, target, sent, came, other in self.messages(j, True):
            copy = remote(source, target, sent, came, device(s, z, other, c))
            copy.start()
            self.started.append(copy)

    def forward(self, j):
        main, tail, pmain, ptail, stage, out_ref = self.refs
        _, _, _, _, zsend, zrecv = self.sems
        s, z, x, c = place()
        half = self.planes // 2
        p = self.pair(j)
        for k in range(2):
            mine = x * self.planes + 2 * p + k
            pmain[mine] = main[mine]
        ptail[x * half + p] = tail[x * half + p]
        for source, target, sent, came, other in self.messages(j, False):
            remote(source, target, sent, came, device(s, z, other, c)).wait_recv()

        def last(source):
            return ptail[source * half + p].astype(F32)

        first, second = last(0) + last(1), last(2) + last(3)
        sections = lax.axis_size("section")
        for k in range(2):
            origin = 2 * p + k

            def piece(source, q):
                return pmain[source * self.planes + origin, q].astype(F32)

            for q in range(QUARTERS):
                stage[origin, q] = (piece(0, q) + piece(1, q)).astype(BF)
                stage[origin, 5 + q] = (piece(2, q) + piece(3, q)).astype(BF)
            stage[origin, 4] = join(first, second, k).astype(BF)
            copy = remote(
                stage.at[origin], out_ref.at[z], zsend.at[2 * j + k], zrecv.at[z],
                device((s + self.by + sections) % sections, origin, x, c),
            )
            copy.start()
            self.started.append(copy)

    def arrive(self):
        stage, out_ref = self.refs[4:]
        zsend, zrecv = self.sems[4:]
        s, z, x, c = place()
        sections = lax.axis_size("section")
        for d in range(self.planes):
            origin = (z + d) % self.planes
            remote(
                stage.at[origin], out_ref.at[origin], zsend.at[d], zrecv.at[origin],
                device((s - self.by + sections) % sections, origin, x, c),
            ).wait_recv()

    def drain(self):
        for copy in self.started:
            copy.wait_send()

    @staticmethod
    def scratch(planes):
        half = planes // 2
        return [
            dma(NX - 1, planes), dma(NX, planes), dma(NX - 1, half), dma(NX, half),
            dma(planes), dma(planes),
        ]


def everyone(planes, sections):
    s, z, x, c = place()
    peers = [device(s, (z + d) % planes, x, c) for d in range(1, planes)]
    peers += [device(s, z, (x + d) % NX, c) for d in range(1, NX)]
    peers += [
        device((s + by) % sections, (z + d) % planes, x, c)
        for by in (1, sections - 1) for d in range(planes)
    ]
    return peers + [device(s, z, x, 1 - c)]


def hand_over(refs, outs, send, recv, target):
    copies = []
    for i, (ref, out) in enumerate(zip(refs, outs)):
        copy = remote(ref, out, send.at[i], recv.at[i], target)
        copy.start()
        copies.append(copy)
    return copies


NAMES = (
    "mid", "grad", "query", "entry", "wide", "down", "expert0", "expert1",
    "kv0", "kv1", "total", "middle", "rows0", "rows1", "rows2", "zbuf0", "zbuf1", "zbuf2", "recv0",
    "recv1", "recv2", "part0", "part1", "pbuf0", "pbuf1", "stage0", "stage1", "back_in",
    "last0", "last1", "last2", "plast0", "plast1", "blast0", "blast1",
    "shared0", "shared1", "shared2",
    "mid_in", "grad_in", "gain_in", "b_meta", "f_meta", "b_meta_in", "result",
)


def main_kernel(
    sel, kv_in, gain, f_route, f_gate, b_route, b_gate,
    mid_hbm, grad_hbm, query_hbm, entry_hbm, wg, wu, wd,
    result_out, middle_out, f_meta_out, front_out,
    *scratch,
):
    v = dict(zip(NAMES, scratch))
    sems = list(scratch[len(NAMES) :])
    s, z, x, c = place()
    sections = lax.axis_size("section")
    planes = v["rows0"].shape[0]
    width = v["rows0"].shape[3]
    experts = planes * 2
    load, csend, crecv, ysend, yrecv = sems[:5]
    sems = sems[5:]
    kv = (v["kv0"], v["kv1"])
    gather = Gather(kv, *sems[:6])
    sends = [
        Dispatch(
            v[f"rows{i}"], v[f"zbuf{i}"], v[f"shared{i}"], v[f"recv{i}"], v[f"last{i}"],
            *sems[6 + 7 * i : 13 + 7 * i],
        )
        for i in range(3)
    ]
    ones, twos, front = sends
    back_ret, front_ret = [
        Return(
            v[f"part{i}"], v[f"plast{i}"], v[f"pbuf{i}"], v[f"blast{i}"], v[f"stage{i}"],
            (v["back_in"], front_out)[i], (-1, 1)[i], *sems[27 + 6 * i : 33 + 6 * i],
        )
        for i in range(2)
    ]

    local = []
    hidden = wg.shape[1]
    places = [v["wide"].at[:, pl.ds(k * hidden, hidden)] for k in range(4)]
    places += [v["down"].at[pl.ds(k * hidden, hidden)] for k in range(2)]
    targets = [v[name] for name in ("mid", "grad", "query", "entry")] + places[::2]
    for i, (source, target) in enumerate(
        zip((mid_hbm, grad_hbm, query_hbm, entry_hbm, wg, wu, wd), targets)
    ):
        copy = pltpu.make_async_copy(source, target, load.at[i])
        copy.start()
        local.append(copy)
    for head in range(KV_HEADS):
        for w in range(2):
            kv[head][c, z, x, w] = kv_in[w * KV_HEADS + head]
    for name, gate_ref, route_ref in (("b_meta", b_gate, b_route), ("f_meta", f_gate, f_route)):
        v[name][...] = jnp.zeros_like(v[name])
        v[name][0:1] = gate_ref[...]
        v[name][1:2] = route_ref[...].astype(F32)
    v["total"][...] = jnp.zeros_like(v["total"])
    greet(everyone(planes, sections))
    stages = stages_of(planes)
    gather.start()
    gather.turn()
    local[0].wait()
    pack(b_route[...], experts, normed_rows(v["mid"], gain, width), v["rows0"])
    ones.send_stages(stages[:1])
    ones.forward(0)
    gate = as_column(b_gate[...])
    local[1].wait()

    def scaled(q):
        return (gate * v["grad"][:, quarter(q, width)].astype(F32)).astype(BF)

    pack(b_route[...], experts, scaled, v["rows1"])
    before = device((s + sections - 1) % sections, z, x, c)
    after = device((s + 1) % sections, z, x, c)
    gather.step(1)
    ones.forward_all(0)
    gather.step(2)
    ones.send_stages(stages[1:2])
    gather.step(3)
    ones.send_stages(stages[2:3])
    gather.step(4)
    ones.send_stages(stages[3:4])
    twos.send_stages(stages)
    twos.forward(0)
    ones.forward_all(1)
    gather.settle()
    shipped = hand_over(
        (v["mid"], v["grad"], gain, v["b_meta"]),
        (v["mid_in"], v["grad_in"], v["gain_in"], v["b_meta_in"]),
        ysend.at[0], yrecv.at[0], before,
    )
    weights = hand_over(
        (wg, wu, wd), places[1::2], csend, crecv,
        device(s, z, x, 1 - c),
    )
    ones.forward_all(2)
    ones.forward_all(3)
    twos.forward_all(0)
    for copy in local[2:4]:
        copy.wait()
    blocks = v["query"].shape[0] // BLK
    first = lax.axis_index("expert") * blocks
    for head in (1, 0):
        gather.ready(head)
        for b in range(blocks):
            attend(b * KV_HEADS + head, first, sel, v["query"], kv, v["total"])
        if head == 1:
            twos.forward_all(1)
    for q in range(QUARTERS):
        cols = quarter(q, width)
        v["middle"][:, cols] = (
            v["entry"][:, cols].astype(F32) + v["total"][:, cols]
        ).astype(BF)
    pack(f_route[...], experts, normed_rows(v["middle"], gain, width), v["rows2"])
    front.send_stages(stages)
    front.forward(0)
    twos.forward_all(2)
    twos.forward_all(3)
    shipped += hand_over(
        (v["middle"], v["f_meta"]), (middle_out, f_meta_out), ysend.at[1], yrecv.at[1], after
    )
    for k in range(len(stages)):
        front.forward_all(k)
    ones.arrive()
    twos.arrive()
    for copy in local[4:]:
        copy.wait()
    for copy in weights:
        copy.wait()
    backward_experts(
        (v["recv0"], v["last0"]), (v["recv1"], v["last1"]), v["expert0"], v["expert1"],
        v["wide"], v["down"], (v["part0"], v["plast0"]),
    )
    turns = back_ret.order()
    flow = Flow([(back_ret, d) for d in turns], 3)
    flow.open()
    front.arrive()
    forward_experts(
        (v["recv2"], v["last2"]), v["expert0"], v["wide"], v["down"], (v["part1"], v["plast1"])
    )
    flow.more([(front_ret, d) for d in turns])
    flow.turn(flow.left() - len(turns) // 2)
    back_ret.arrive()
    for copy in shipped:
        copy.wait()
    back_last(
        v["mid_in"], v["grad_in"], v["gain_in"], v["back_in"], v["b_meta_in"],
        v["result"], v["total"],
    )
    last = pltpu.make_async_copy(v["result"], result_out, load.at[7])
    last.start()
    flow.turn(flow.left())
    front_ret.arrive()
    last.wait()
    for one in (gather, ones, twos, front, back_ret, front_ret):
        one.drain()


ANY = pl.BlockSpec(memory_space=pl.ANY)
VMEM = pl.BlockSpec(memory_space=pltpu.VMEM)
SMEM = pl.BlockSpec(memory_space=pltpu.SMEM)


def shards(
    front_input, queries, keys_values, selected_blocks, front_route, front_gate,
    back_middle, back_grad, back_route, back_gate, norm_gain, gate_slice, up_slice, down_slice,
):
    tokens, features = front_input.shape[1:]
    planes = lax.axis_size("expert") // (2 * NX)
    width = features // QUARTERS
    kv = keys_values[0].T.reshape(2 * KV_HEADS, HEAD_DIM, tokens)
    message = pltpu.VMEM((planes, 9, 8, width), BF)
    arrived = pltpu.VMEM((NX * planes, QUARTERS, 8, width), BF)
    lasts = pltpu.VMEM((NX * planes // 2, 8, width), BF)
    rows = pltpu.VMEM((tokens, features), BF)
    many = pltpu.VMEM((NX * planes * 9, features), BF)
    meta = pltpu.VMEM((8, tokens), F32)
    half_kv = pltpu.VMEM((2, planes, NX, 2, HEAD_DIM, tokens), BF)
    shapes = dict(
        mid=rows, grad=rows, query=rows, entry=rows,
        wide=pltpu.VMEM((features, 4 * gate_slice.shape[3]), BF),
        down=pltpu.VMEM((2 * gate_slice.shape[3], features), BF),
        expert0=many, expert1=many, kv0=half_kv, kv1=half_kv,
        total=pltpu.VMEM((tokens, features), F32), middle=rows,
        back_in=message, mid_in=rows, grad_in=rows, gain_in=pltpu.VMEM((1, features), F32),
        b_meta=meta, f_meta=meta, b_meta_in=meta, result=rows,
    )
    for i in range(3):
        shapes[f"rows{i}"] = shapes[f"zbuf{i}"] = message
        shapes[f"recv{i}"] = shapes[f"part{i}"] = shapes[f"pbuf{i}"] = arrived
        shapes[f"stage{i}"] = message
        shapes[f"last{i}"] = shapes[f"plast{i}"] = shapes[f"blast{i}"] = lasts
        shapes[f"shared{i}"] = pltpu.VMEM((planes // 2, 2, 8, width), BF)
    result, middle, f_meta, front = pl.pallas_call(
        main_kernel,
        out_shape=[
            jax.ShapeDtypeStruct((tokens, features), BF),
            jax.ShapeDtypeStruct((tokens, features), BF),
            jax.ShapeDtypeStruct((8, tokens), F32),
            jax.ShapeDtypeStruct((planes, 9, 8, width), BF),
        ],
        in_specs=[SMEM] + [VMEM] * 6 + [ANY] * 7,
        out_specs=[ANY] * 4,
        scratch_shapes=[shapes[name] for name in NAMES]
        + [dma(8), dma(3), dma(3), dma(2, 4), dma(2, 4)]
        + Gather.scratch(planes) + Dispatch.scratch(planes) * 3 + Return.scratch(planes) * 2,
        compiler_params=pltpu.CompilerParams(
            collective_id=0, has_side_effects=True, vmem_limit_bytes=63 << 20
        ),
        name="layer",
    )(
        selected_blocks[0], kv, norm_gain,
        front_route.reshape(1, tokens), front_gate.reshape(1, tokens),
        back_route.reshape(1, tokens), back_gate.reshape(1, tokens),
        back_middle[0], back_grad[0], queries[0], front_input[0],
        gate_slice[0, 0], up_slice[0, 0], down_slice[0, 0],
    )
    front_output, back_output = pl.pallas_call(
        front_last_kernel,
        out_shape=[jax.ShapeDtypeStruct((tokens, features), BF)] * 2,
        in_specs=[ANY] * 4,
        out_specs=[ANY] * 2,
        scratch_shapes=[rows, message, meta, rows, rows, dma(5 + QUARTERS)],
        compiler_params=pltpu.CompilerParams(vmem_limit_bytes=63 << 20),
        name="front_last",
    )(middle, front, f_meta, result)
    return (front_output[None], back_output[None])


def solution(mesh):
    rows = P("section", "expert", None)
    wide = P("section", "expert", None, None)
    return jax.shard_map(
        shards,
        mesh=mesh,
        in_specs=(rows, rows, rows, wide, rows, rows, rows, rows, rows, rows,
                  P("section", None), wide, wide, wide),
        out_specs=(rows, rows),
        check_vma=False,
    )
```
